256 devices in a mesh: expert: 2 (over z_lo), batch: 4 (over x), seq: 32 (over y, z_hi, core).
Axes of the slice: x: 4, y: 4, z: 8 (z_hi: 4, z_lo: 2; z = z_hi * 2 + z_lo), core: 2. Of those that a mesh axis runs over, the one named last changes fastest.
Arguments:
- queries: bfloat16 [2, 4, 2, 3072, 4096], P('expert', 'batch', None, 'seq'), may hold values from -36 to 36
- keys: bfloat16 [2, 4, 2, 3072, 4096], P('expert', 'batch', None, 'seq'), may hold values from -21 to 21
- values: bfloat16 [2, 4, 2, 3072, 4096], P('expert', 'batch', None, 'seq'), may hold values from -6 to 6
- latents: bfloat16 [2, 4, 3072, 4096], P('expert', 'batch', 'seq'), may hold values from -6 to 6
- gain: bfloat16 [2, 4096], P('expert'), may hold values from 0.099609375 to 1.8984375
- steps_table: int32 [2, 4], P('expert', 'batch'), may hold values from 0 to 38
- flags: int32 [4], P('batch'), may hold values 0 or 1
Outputs:
- denoised: bfloat16 [2, 4, 3072, 4096], P('expert', 'batch', 'seq')
- next_latents: bfloat16 [2, 4, 3072, 4096], P('expert', 'batch', 'seq')
The draws below stay inside these ranges and needn't reach their ends.
All inputs are finite; a program needn't handle non-finite values. No bound on the sum of `flags` on one device may be relied on, other than what follows from the above.
Results may differ from the reference program's by a relative error of at most 0.006.
Values may be sent and summed in bfloat16 or wider, within the bound.
No kernel may reach another device: no remote copies, remote signals or barrier semaphores. Data moves between devices by JAX's collectives and lax.ppermute only.
A program may use at most 64 MiB of HBM per device.

```python
import jax
import jax.numpy as jnp
from jax import lax

HEADS = 32
HDIM = 128
STEPS = 40
BOUNDARY = 15
BATCH = 4
SEQ = 3072
WIDTH = 4096


def paired_draw(key):
    base = jax.random.fold_in(key, 7)
    query_key, key_key = jax.random.split(base, 2)
    shape = (2, BATCH, 2, SEQ, HEADS * HDIM)
    query_part = jnp.clip(jax.random.normal(query_key, shape, jnp.float32), -5.0, 5.0)
    key_part = jnp.clip(jax.random.normal(key_key, shape, jnp.float32), -5.0, 5.0)
    return (query_part, key_part)


def draw_queries(key, part):
    return paired_draw(key)[0].astype(jnp.bfloat16)


def draw_keys(key, part):
    return paired_draw(key)[1].astype(jnp.bfloat16)


def draw_steps_table(key, part):
    base = jax.random.fold_in(key, 11)
    high_key, low_key, high_pick, low_pick = jax.random.split(base, 4)
    high_steps = jax.random.randint(high_key, (BATCH,), 0, BOUNDARY)
    low_steps = jax.random.randint(low_key, (BATCH,), BOUNDARY, STEPS - 1)
    places = jnp.arange(BATCH, dtype=jnp.int32)
    high_spot = jax.random.randint(high_pick, (), 0, BATCH)
    low_spot = jax.random.randint(low_pick, (), 0, BATCH)
    high_steps = jnp.where(places == high_spot, 0, high_steps)
    low_steps = jnp.where(places == low_spot, STEPS - 2, low_steps)
    return jnp.stack([high_steps, low_steps], axis=0).astype(jnp.int32)


def touch_ends(values, stream_key, low, largest):
    longest = values.shape.index(max(values.shape))
    spots = []
    for shift in (0, 1):
        where = [jax.random.randint(jax.random.fold_in(stream_key, axis), (), 0, length) for axis, length in enumerate(values.shape)]
        where[longest] = (where[longest] + shift) % values.shape[longest]
        spots.append(tuple(where))
    return values.at[spots[0]].set(low).at[spots[1]].set(largest)


def levels(stream_key, extent, shards, least, high):
    level, own = 1.0, jax.random.fold_in(stream_key, 6)
    for axis_at, parts in shards:
        heights = jnp.exp(jax.random.uniform(jax.random.fold_in(own, axis_at), (parts,), jnp.float32, least / len(shards), high / len(shards)))
        level = level * jnp.repeat(heights, extent[axis_at] // parts).reshape([-1 if axis == axis_at else 1 for axis in range(len(extent))])
    return level


def gaussian(rng, extent, scale, most, cuts=(), kind=jnp.bfloat16):
    result = scale * jax.random.normal(rng, extent, jnp.float32)
    if cuts:
        result = result * levels(rng, extent, cuts, -0.22, 0.18)
    return jnp.clip(result, -most, most).astype(kind)


def setup_inputs(seed: int = 0) -> dict:
    seeds = jax.random.split(jax.random.key(seed), 8)
    queries = draw_queries(jax.random.fold_in(seeds[7], 71), 0)
    keys = draw_keys(jax.random.fold_in(seeds[7], 71), 0)
    values = gaussian(seeds[2], (2, BATCH, 2, SEQ, WIDTH), 1.0, 6.0, ((0, 2), (1, 4), (3, 32)))
    latents = gaussian(seeds[3], (2, BATCH, SEQ, WIDTH), 1.0, 6.0, ((0, 2), (1, 4), (2, 32)))
    gain = jnp.clip(1.0 + 0.18 * jax.random.normal(seeds[4], (2, WIDTH), jnp.float32), 0.099609375, 1.8984375).astype(jnp.bfloat16)
    steps_table = draw_steps_table(jax.random.fold_in(seeds[7], 71), 0)
    flags = touch_ends((jax.random.randint(seeds[6], (BATCH,), 0, 2) < 1).astype(jnp.int32), jax.random.fold_in(seeds[6], 1), 0, 1)
    return dict(queries=queries, keys=keys, values=values, latents=latents, gain=gain, steps_table=steps_table, flags=flags)


GUIDANCE = 3.5
flow_shift = 5.0

def sigma_of(step):
    level = 1.0 - step.astype(jnp.float32) / STEPS
    return flow_shift * level / (1.0 + (flow_shift - 1.0) * level)

def attend_head(query, key_rows, value_rows):
    scores = jnp.dot(query, key_rows.T, preferred_element_type=jnp.float32) * HDIM ** (-0.5)
    weights = jax.nn.softmax(scores, axis=-1).astype(jnp.bfloat16)
    return jnp.dot(weights, value_rows, preferred_element_type=jnp.float32).astype(jnp.bfloat16)

def combine(cond, uncond):
    base = uncond.astype(jnp.float32)
    return (base + GUIDANCE * (cond.astype(jnp.float32) - base)).astype(jnp.bfloat16)

def reference(queries, keys, values, latents, gain, steps_table, flags):
    groups, clips, branches, length, width = queries.shape

    def heads_first(array):
        shaped = array.reshape(groups * clips * branches, length, HEADS, HDIM)
        return shaped.transpose(0, 2, 1, 3).reshape(-1, length, HDIM)
    outcome = lax.map(lambda triple: attend_head(*triple), (heads_first(queries), heads_first(keys), heads_first(values)))
    attended = outcome.reshape(groups, clips, branches, HEADS, length, HDIM)
    attended = attended.transpose(0, 1, 2, 4, 3, 5).reshape(groups, clips, branches, length, width)
    guided = combine(attended[:, :, 0], attended[:, :, 1]).astype(jnp.float32)
    scale = lax.rsqrt(lax.optimization_barrier(jnp.mean(guided * guided, axis=-1, keepdims=True)) + 1e-06)
    velocity = guided * scale * gain.astype(jnp.float32)[:, None, None, :]
    sigma_now = sigma_of(steps_table)[:, :, None, None]
    sigma_next = sigma_of(steps_table + 1)[:, :, None, None]
    current = latents.astype(jnp.float32)
    denoised = (current - sigma_now * velocity).astype(jnp.bfloat16)
    moved = (current + (sigma_next - sigma_now) * velocity).astype(jnp.bfloat16)
    crossing = (flags == 1)[None, :, None, None]
    next_latents = jnp.where(crossing, moved[::-1], moved)
    return (denoised, next_latents)
```

```python
import functools
import math

import jax
import jax.numpy as jnp
from jax import lax
from jax.experimental import pallas as pl
from jax.experimental.pallas import tpu as pltpu
from jax.sharding import PartitionSpec as P

HDIM = 128
STEPS = 40
GUIDANCE = 3.5
FLOW_SHIFT = 5.0
BF16 = jnp.bfloat16
F32 = jnp.float32

PARTS = 2
LOG2_SCALE = math.log2(math.e) / math.sqrt(HDIM)
SAFE_LOG2 = 100.0
CONTRACT_LAST = (((1,), (1,)), ((), ()))
VMEM_LIMIT = 56 << 20


def sigma_of(step):
    level = 1.0 - step.astype(F32) / STEPS
    return FLOW_SHIFT * level / (1.0 + (FLOW_SHIFT - 1.0) * level)


def pack_kernel(*refs, heads):
    *sources, out = refs
    for h in range(heads):
        columns = slice(h * HDIM, (h + 1) * HDIM)
        at = 0
        for source in sources:
            for branch in range(2):
                out[h, at] = source[0, 0, branch, :, columns]
                at += 1


def pack(sources, first_row, rows, heads_per_step=8):
    width = sources[0].shape[-1]
    heads = width // HDIM
    block = first_row // rows
    return pl.pallas_call(
        functools.partial(pack_kernel, heads=heads_per_step),
        grid=(heads // heads_per_step,),
        in_specs=[
            pl.BlockSpec((1, 1, 2, rows, heads_per_step * HDIM), lambda i: (0, 0, 0, block, i))
            for _ in sources
        ],
        out_specs=pl.BlockSpec((heads_per_step, 2 * len(sources), rows, HDIM), lambda i: (i, 0, 0, 0)),
        out_shape=jax.ShapeDtypeStruct((heads, 2 * len(sources), rows, HDIM), BF16),
        compiler_params=pltpu.CompilerParams(vmem_limit_bytes=VMEM_LIMIT),
    )(*sources)


def attend_kernel(q_ref, kv_ref, o_ref, k_sc, v_sc, norm_sc, *, block):
    peers, _, shard, _ = kv_ref.shape
    keys = peers * shard
    groups, _, part, _ = q_ref.shape
    rows = groups * part
    blocks = keys // block

    @pl.when(pl.program_id(0) == 0)
    def _():
        for c in range(2):
            k = kv_ref[:, c].reshape(keys, HDIM)
            k_f32 = k.astype(F32)
            norm_sc[c] = jnp.max(jnp.sum(k_f32 * k_f32, axis=1, keepdims=True))
            k_sc[c, :, :HDIM] = k
            k_sc[c, :, HDIM:] = k
            v_sc[c, :, :HDIM] = kv_ref[:, 2 + c].reshape(keys, HDIM)
            v_sc[c, :, HDIM:] = jnp.ones((keys, HDIM), BF16)

    scaled, bound = [], 0.0
    for c in range(2):
        q = q_ref[:, c].reshape(rows, HDIM).astype(F32) * LOG2_SCALE
        high = q.astype(BF16)
        low = (q - high.astype(F32)).astype(BF16)
        scaled.append(jnp.concatenate([high, low], axis=1))
        bound = jnp.maximum(bound, jnp.max(jnp.sum(q * q, axis=1, keepdims=True)) * norm_sc[c])
    unshifted = bound <= SAFE_LOG2 * SAFE_LOG2

    def scores(c, j):
        return lax.dot_general(
            scaled[c], k_sc[c, pl.ds(j * block, block), :], CONTRACT_LAST, preferred_element_type=F32
        )

    def weigh(c, j, weights):
        return jnp.dot(weights.astype(BF16), v_sc[c, pl.ds(j * block, block), :], preferred_element_type=F32)

    def finish(sums):
        cond, uncond = (s[:, :HDIM] / s[:, HDIM:] for s in sums)
        o_ref[...] = (uncond + GUIDANCE * (cond - uncond)).astype(BF16).reshape(groups, part, HDIM)

    @pl.when(unshifted)
    def _():
        order = [(c, j) for c in range(2) for j in range(blocks)]
        sums = [None, None]
        ahead = scores(*order[0])
        for i, (c, j) in enumerate(order):
            now = ahead
            if i + 1 < len(order):
                ahead = scores(*order[i + 1])
            part_sum = weigh(c, j, jnp.exp2(now))
            sums[c] = part_sum if sums[c] is None else sums[c] + part_sum
        finish(sums)

    @pl.when(jnp.logical_not(unshifted))
    def _():
        sums = []
        for c in range(2):
            top = lax.fori_loop(
                0,
                blocks,
                lambda j, m: jnp.maximum(m, jnp.max(scores(c, j), axis=1, keepdims=True)),
                jnp.full((rows, 1), -jnp.inf, F32),
            )
            sums.append(
                lax.fori_loop(
                    0,
                    blocks,
                    lambda j, acc: acc + weigh(c, j, jnp.exp2(scores(c, j) - top)),
                    jnp.zeros((rows, 2 * HDIM), F32),
                )
            )
        finish(sums)


def attend(q, kv, groups=16, block=256):
    peers, _, part, _ = q.shape
    keys = kv.shape[0] * kv.shape[2]
    return pl.pallas_call(
        functools.partial(attend_kernel, block=block),
        grid=(peers // groups,),
        in_specs=[
            pl.BlockSpec((groups, 2, part, HDIM), lambda i: (i, 0, 0, 0)),
            pl.BlockSpec(kv.shape, lambda i: (0, 0, 0, 0), pipeline_mode=pl.Buffered(1)),
        ],
        out_specs=pl.BlockSpec((groups, part, HDIM), lambda i: (i, 0, 0)),
        out_shape=jax.ShapeDtypeStruct((peers, part, HDIM), BF16),
        scratch_shapes=[
            pltpu.VMEM((2, keys, 2 * HDIM), BF16),
            pltpu.VMEM((2, keys, 2 * HDIM), BF16),
            pltpu.SMEM((2,), F32),
        ],
        compiler_params=pltpu.CompilerParams(vmem_limit_bytes=VMEM_LIMIT),
    )(q, kv)


def step_kernel(sigmas, guided, latents, gain, *outs):
    denoised, moved = outs[-2:]
    heads = guided.shape[0]
    total = None
    for h in range(heads):
        g = guided[h].astype(F32)
        total = g * g if total is None else total + g * g
    mean = jnp.sum(total, axis=1, keepdims=True) / (heads * HDIM)
    scale = lax.rsqrt(mean + 1e-06)
    for h in range(heads):
        columns = slice(h * HDIM, (h + 1) * HDIM)
        velocity = guided[h].astype(F32) * scale * gain[:, columns].astype(F32)
        current = latents[0, 0, :, columns].astype(F32)
        denoised[0, 0, :, columns] = (current - sigmas[0] * velocity).astype(BF16)
        moved[:, columns] = (current + sigmas[1] * velocity).astype(BF16)


def sample_step(part, sigmas, guided, latents, gain, denoised):
    heads, rows, _ = guided.shape
    width = heads * HDIM
    rows_spec = pl.BlockSpec((1, 1, rows, width), lambda i: (0, 0, part, 0))
    operands = [sigmas, guided, latents, gain]
    in_specs = [
        pl.BlockSpec(memory_space=pltpu.SMEM),
        pl.BlockSpec((heads, rows, HDIM), lambda i: (0, 0, 0)),
        rows_spec,
        pl.BlockSpec((1, width), lambda i: (0, 0)),
    ]
    aliases = {}
    kernel = step_kernel
    if denoised is not None:
        operands.append(denoised)
        in_specs.append(pl.BlockSpec(memory_space=pl.ANY))
        aliases = {4: 0}
    return pl.pallas_call(
        kernel,
        grid=(1,),
        in_specs=in_specs,
        out_specs=[rows_spec, pl.BlockSpec((rows, width), lambda i: (0, 0))],
        out_shape=[
            jax.ShapeDtypeStruct(latents.shape, BF16),
            jax.ShapeDtypeStruct((rows, width), BF16),
        ],
        input_output_aliases=aliases,
        compiler_params=pltpu.CompilerParams(vmem_limit_bytes=VMEM_LIMIT),
    )(*operands)


def per_device(queries, keys, values, latents, gain, steps_table, flags):
    tokens = queries.shape[3]
    rows = tokens // PARTS
    swap = lambda a: lax.all_to_all(a, "seq", split_axis=0, concat_axis=0, tiled=True)
    kv = swap(pack((keys, values), 0, tokens))
    q = [swap(pack((queries,), p * rows, rows)) for p in range(PARTS)]
    guided = [swap(attend(q[p], kv)) for p in range(PARTS)]

    step_now = steps_table[0, 0]
    sigma_now = sigma_of(step_now)
    sigmas = jnp.stack([sigma_now, sigma_of(step_now + 1) - sigma_now])
    denoised, moved, partner = None, [], []
    for p in range(PARTS):
        denoised, part = sample_step(p, sigmas, guided[p], latents, gain, denoised)
        moved.append(part)
        partner.append(lax.ppermute(part, "expert", [(0, 1), (1, 0)]))
    trade = flags[0] == 1
    next_latents = jnp.concatenate([jnp.where(trade, a, b) for a, b in zip(partner, moved)], axis=0)
    return (denoised, next_latents[None, None])


def solution(mesh):
    placed = (
        P("expert", "batch", None, "seq", None),
        P("expert", "batch", None, "seq", None),
        P("expert", "batch", None, "seq", None),
        P("expert", "batch", "seq", None),
        P("expert", None),
        P("expert", "batch"),
        P("batch"),
    )
    return jax.shard_map(
        per_device,
        mesh=mesh,
        in_specs=placed,
        out_specs=(P("expert", "batch", "seq", None), P("expert", "batch", "seq", None)),
        check_vma=False,
    )
```

```python
import functools
import math

import jax
import jax.numpy as jnp
from jax import lax
from jax.experimental import pallas as pl
from jax.experimental.pallas import tpu as pltpu
from jax.sharding import PartitionSpec as P

HDIM = 128
STEPS = 40
GUIDANCE = 3.5
FLOW_SHIFT = 5.0
BF16 = jnp.bfloat16
F32 = jnp.float32

LOG2_SCALE = math.log2(math.e) / math.sqrt(HDIM)
SAFE_LOG2 = 100.0
CONTRACT_LAST = (((1,), (1,)), ((), ()))
VMEM_LIMIT = 56 << 20


def sigma_of(step):
    level = 1.0 - step.astype(F32) / STEPS
    return FLOW_SHIFT * level / (1.0 + (FLOW_SHIFT - 1.0) * level)


def pack_kernel(*refs, spans):
    count = len(spans)
    sources, out, (ins, outs, in_sems, out_sems) = refs[:count], refs[count], refs[count + 1 :]
    heads = out.shape[0]
    pieces, at = [], 0
    for source, (first, rows) in zip(sources, spans):
        for branch in range(2):
            pieces.append((source.at[0, 0, branch, pl.ds(first, rows)], at, rows))
            at += rows
    reads = [
        pltpu.make_async_copy(source, ins.at[pl.ds(at, rows)], in_sems.at[n])
        for n, (source, at, rows) in enumerate(pieces)
    ]
    writes = [
        pltpu.make_async_copy(outs.at[:, pl.ds(at, rows)], out.at[:, pl.ds(at, rows)], out_sems.at[n])
        for n, (_, at, rows) in enumerate(pieces)
    ]
    for read in reads:
        read.start()
    for (_, at, rows), read, write in zip(pieces, reads, writes):
        read.wait()
        for h in range(heads):
            outs[h, at : at + rows] = ins[at : at + rows, h * HDIM : (h + 1) * HDIM]
        write.start()
    for write in writes:
        write.wait()


def pack(sources, spans):
    width = sources[0].shape[-1]
    heads = width // HDIM
    total = sum(2 * rows for _, rows in spans)
    count = 2 * len(spans)
    return pl.pallas_call(
        functools.partial(pack_kernel, spans=spans),
        in_specs=[pl.BlockSpec(memory_space=pl.ANY) for _ in sources],
        out_specs=pl.BlockSpec(memory_space=pl.ANY),
        out_shape=jax.ShapeDtypeStruct((heads, total, HDIM), BF16),
        scratch_shapes=[
            pltpu.VMEM((total, width), BF16),
            pltpu.VMEM((heads, total, HDIM), BF16),
            pltpu.SemaphoreType.DMA((count,)),
            pltpu.SemaphoreType.DMA((count,)),
        ],
        compiler_params=pltpu.CompilerParams(vmem_limit_bytes=VMEM_LIMIT),
    )(*sources)


def attend_kernel(*refs, shard, part, first, groups, block):
    kv_ref, q_ref = refs[0], refs[-5]
    o_ref, k_sc, v_sc, norm_sc = refs[-4:]
    keys = kv_ref.shape[0] * shard
    rows = groups * part
    blocks = keys // block

    def resident(n):
        return kv_ref[:, n * shard : (n + 1) * shard].reshape(keys, HDIM)

    @pl.when(pl.program_id(0) == 0)
    def _():
        for c in range(2):
            k = resident(c)
            k_f32 = k.astype(F32)
            norm_sc[c] = jnp.max(jnp.sum(k_f32 * k_f32, axis=1, keepdims=True))
            k_sc[c, :, :HDIM] = k
            k_sc[c, :, HDIM:] = k
            v_sc[c, :, :HDIM] = resident(2 + c)
            v_sc[c, :, HDIM:] = jnp.ones((keys, HDIM), BF16)

    here = pl.ds(pl.program_id(0) * groups, groups)
    scaled, bound = [], 0.0
    for c in range(2):
        own = slice(first + c * part, first + (c + 1) * part)
        q = q_ref[here, own].reshape(rows, HDIM).astype(F32) * LOG2_SCALE
        high = q.astype(BF16)
        low = (q - high.astype(F32)).astype(BF16)
        scaled.append(jnp.concatenate([high, low], axis=1))
        bound = jnp.maximum(bound, jnp.max(jnp.sum(q * q, axis=1, keepdims=True)) * norm_sc[c])
    unshifted = bound <= SAFE_LOG2 * SAFE_LOG2

    def scores(c, j):
        return lax.dot_general(
            scaled[c], k_sc[c, pl.ds(j * block, block), :], CONTRACT_LAST, preferred_element_type=F32
        )

    def weigh(c, j, weights):
        return jnp.dot(weights.astype(BF16), v_sc[c, pl.ds(j * block, block), :], preferred_element_type=F32)

    def finish(sums):
        cond, uncond = (s[:, :HDIM] / s[:, HDIM:] for s in sums)
        o_ref[...] = (uncond + GUIDANCE * (cond - uncond)).astype(BF16).reshape(groups, part, HDIM)

    @pl.when(unshifted)
    def _():
        order = [(c, j) for c in range(2) for j in range(blocks)]
        sums = [None, None]
        ahead = scores(*order[0])
        for i, (c, j) in enumerate(order):
            now = ahead
            if i + 1 < len(order):
                ahead = scores(*order[i + 1])
            part_sum = weigh(c, j, jnp.exp2(now))
            sums[c] = part_sum if sums[c] is None else sums[c] + part_sum
        finish(sums)

    @pl.when(jnp.logical_not(unshifted))
    def _():
        sums = []
        for c in range(2):
            top = lax.fori_loop(
                0,
                blocks,
                lambda j, m: jnp.maximum(m, jnp.max(scores(c, j), axis=1, keepdims=True)),
                jnp.full((rows, 1), -jnp.inf, F32),
            )
            sums.append(
                lax.fori_loop(
                    0,
                    blocks,
                    lambda j, acc: acc + weigh(c, j, jnp.exp2(scores(c, j) - top)),
                    jnp.zeros((rows, 2 * HDIM), F32),
                )
            )
        finish(sums)


def attend(arrays, shard, part, first, groups, block=256):
    peers = arrays[0].shape[0]
    keys = peers * shard
    return pl.pallas_call(
        functools.partial(attend_kernel, shard=shard, part=part, first=first, groups=groups, block=block),
        grid=(peers // groups,),
        in_specs=[
            pl.BlockSpec(a.shape, lambda i: (0, 0, 0), pipeline_mode=pl.Buffered(1)) for a in arrays
        ],
        out_specs=pl.BlockSpec((groups, part, HDIM), lambda i: (i, 0, 0)),
        out_shape=jax.ShapeDtypeStruct((peers, part, HDIM), BF16),
        scratch_shapes=[
            pltpu.VMEM((2, keys, 2 * HDIM), BF16),
            pltpu.VMEM((2, keys, 2 * HDIM), BF16),
            pltpu.SMEM((2,), F32),
        ],
        compiler_params=pltpu.CompilerParams(vmem_limit_bytes=VMEM_LIMIT),
    )(*arrays)


def step_kernel(steps, guided, latents, gain, *outs):
    denoised, moved = outs[-2:]
    heads = guided.shape[0]
    sigma_now = sigma_of(steps[0, 0])
    sigma_change = sigma_of(steps[0, 0] + 1) - sigma_now
    total = None
    for h in range(heads):
        g = guided[h].astype(F32)
        total = g * g if total is None else total + g * g
    mean = jnp.sum(total, axis=1, keepdims=True) / (heads * HDIM)
    scale = lax.rsqrt(mean + 1e-06)
    for h in range(heads):
        columns = slice(h * HDIM, (h + 1) * HDIM)
        velocity = guided[h].astype(F32) * scale * gain[:, columns].astype(F32)
        current = latents[0, 0, :, columns].astype(F32)
        denoised[0, 0, :, columns] = (current - sigma_now * velocity).astype(BF16)
        moved[:, columns] = (current + sigma_change * velocity).astype(BF16)


def token_rows(first, rows, width):
    return pl.BlockSpec((1, 1, rows, width), lambda i: (0, 0, first // rows, 0))


def sample_step(first, steps_table, guided, latents, gain, before):
    heads, rows, _ = guided.shape
    width = heads * HDIM
    return pl.pallas_call(
        step_kernel,
        grid=(1,),
        in_specs=[
            pl.BlockSpec(memory_space=pltpu.SMEM),
            pl.BlockSpec((heads, rows, HDIM), lambda i: (0, 0, 0)),
            token_rows(first, rows, width),
            pl.BlockSpec((1, width), lambda i: (0, 0)),
        ]
        + [pl.BlockSpec(memory_space=pl.ANY) for _ in before],
        out_specs=[token_rows(first, rows, width), pl.BlockSpec((rows, width), lambda i: (0, 0))],
        out_shape=[
            jax.ShapeDtypeStruct(latents.shape, BF16),
            jax.ShapeDtypeStruct((rows, width), BF16),
        ],
        input_output_aliases={4: 0} if before else {},
        compiler_params=pltpu.CompilerParams(vmem_limit_bytes=VMEM_LIMIT),
    )(steps_table, guided, latents, gain, *before)


def choose_kernel(flags, partner, moved, *outs):
    outs[-1][0, 0] = jnp.where(flags[0] == 1, partner[...], moved[...])


def choose(first, flags, partner, moved, shape, before):
    rows, width = moved.shape
    whole = pl.BlockSpec((rows, width), lambda i: (0, 0))
    return pl.pallas_call(
        choose_kernel,
        grid=(1,),
        in_specs=[pl.BlockSpec(memory_space=pltpu.SMEM), whole, whole]
        + [pl.BlockSpec(memory_space=pl.ANY) for _ in before],
        out_specs=token_rows(first, rows, width),
        out_shape=jax.ShapeDtypeStruct(shape, BF16),
        input_output_aliases={3: 0} if before else {},
        compiler_params=pltpu.CompilerParams(vmem_limit_bytes=VMEM_LIMIT),
    )(flags, partner, moved, *before)


def per_device(queries, keys, values, latents, gain, steps_table, flags):
    tokens = queries.shape[3]
    head, tail = tokens - tokens // 3, tokens // 3
    exchange = lambda a: lax.all_to_all(a, "seq", split_axis=0, concat_axis=0, tiled=True)
    after = lambda a, done: lax.optimization_barrier((a, done))[0]
    kvq = exchange(pack((keys, values, queries), ((0, tokens), (0, tokens), (0, head))))
    rest = exchange(after(pack((queries,), ((head, tail),)), kvq))
    guided_head = exchange(after(attend((kvq,), tokens, head, 4 * tokens, groups=8), rest))
    own_tail = attend((kvq, rest), tokens, tail, 0, groups=16)
    guided_head, own_tail = lax.optimization_barrier((guided_head, own_tail))
    guided_tail = exchange(own_tail)

    swap = lambda a: lax.ppermute(a, "expert", [(0, 1), (1, 0)])
    denoised, moved_head = sample_step(0, steps_table, guided_head, latents, gain, ())
    partner_head = swap(moved_head)
    denoised, moved_tail = sample_step(
        head, steps_table, guided_tail, latents, gain, (denoised, partner_head)
    )
    partner_tail = swap(moved_tail)
    next_latents = choose(0, flags, partner_head, moved_head, latents.shape, ())
    next_latents = choose(head, flags, partner_tail, moved_tail, latents.shape, (next_latents,))
    return (denoised, next_latents)


def solution(mesh):
    placed = (
        P("expert", "batch", None, "seq", None),
        P("expert", "batch", None, "seq", None),
        P("expert", "batch", None, "seq", None),
        P("expert", "batch", "seq", None),
        P("expert", None),
        P("expert", "batch"),
        P("batch"),
    )
    return jax.shard_map(
        per_device,
        mesh=mesh,
        in_specs=placed,
        out_specs=(P("expert", "batch", "seq", None), P("expert", "batch", "seq", None)),
        check_vma=False,
    )
```

```python
import functools
import math

import jax
import jax.numpy as jnp
from jax import lax
from jax.experimental import pallas as pl
from jax.experimental.pallas import tpu as pltpu
from jax.sharding import PartitionSpec as P

HDIM = 128
STEPS = 40
GUIDANCE = 3.5
FLOW_SHIFT = 5.0
BF16 = jnp.bfloat16
F32 = jnp.float32

LOG2_SCALE = math.log2(math.e) / math.sqrt(HDIM)
SAFE_LOG2 = 100.0
CONTRACT_LAST = (((1,), (1,)), ((), ()))
VMEM_LIMIT = 56 << 20


def sigma_of(step):
    level = 1.0 - step.astype(F32) / STEPS
    return FLOW_SHIFT * level / (1.0 + (FLOW_SHIFT - 1.0) * level)


def pack_kernel(*refs, spans):
    count = len(spans)
    sources, out, (ins, outs, in_sems, out_sems) = refs[:count], refs[count], refs[count + 1 :]
    heads = out.shape[0]
    pieces, at = [], 0
    for source, (first, rows) in zip(sources, spans):
        for branch in range(2):
            pieces.append((source.at[0, 0, branch, pl.ds(first, rows)], at, rows))
            at += rows
    reads = [
        pltpu.make_async_copy(source, ins.at[pl.ds(at, rows)], in_sems.at[n])
        for n, (source, at, rows) in enumerate(pieces)
    ]
    writes = [
        pltpu.make_async_copy(outs.at[:, pl.ds(at, rows)], out.at[:, pl.ds(at, rows)], out_sems.at[n])
        for n, (_, at, rows) in enumerate(pieces)
    ]
    for read in reads:
        read.start()
    for (_, at, rows), read, write in zip(pieces, reads, writes):
        read.wait()
        for h in range(heads):
            outs[h, at : at + rows] = ins[at : at + rows, h * HDIM : (h + 1) * HDIM]
        write.start()
    for write in writes:
        write.wait()


def pack(sources, spans):
    width = sources[0].shape[-1]
    heads = width // HDIM
    total = sum(2 * rows for _, rows in spans)
    count = 2 * len(spans)
    return pl.pallas_call(
        functools.partial(pack_kernel, spans=spans),
        in_specs=[pl.BlockSpec(memory_space=pl.ANY) for _ in sources],
        out_specs=pl.BlockSpec(memory_space=pl.ANY),
        out_shape=jax.ShapeDtypeStruct((heads, total, HDIM), BF16),
        scratch_shapes=[
            pltpu.VMEM((total, width), BF16),
            pltpu.VMEM((heads, total, HDIM), BF16),
            pltpu.SemaphoreType.DMA((count,)),
            pltpu.SemaphoreType.DMA((count,)),
        ],
        compiler_params=pltpu.CompilerParams(vmem_limit_bytes=VMEM_LIMIT),
    )(*sources)


def attend_kernel(*refs, arrays, shard, part, first, groups, block):
    kv_ref, q_ref = refs[0], refs[arrays - 1]
    o_ref, k_sc, v_sc, norm_sc = refs[-4:]
    keys = kv_ref.shape[0] * shard
    rows = groups * part
    blocks = keys // block

    def resident(n):
        return kv_ref[:, n * shard : (n + 1) * shard].reshape(keys, HDIM)

    @pl.when(pl.program_id(0) == 0)
    def _():
        for c in range(2):
            k = resident(c)
            k_f32 = k.astype(F32)
            norm_sc[c] = jnp.max(jnp.sum(k_f32 * k_f32, axis=1, keepdims=True))
            k_sc[c, :, :HDIM] = k
            k_sc[c, :, HDIM:] = k
            v_sc[c, :, :HDIM] = resident(2 + c)
            v_sc[c, :, HDIM:] = jnp.ones((keys, HDIM), BF16)

    here = pl.ds(pl.program_id(0) * groups, groups)
    scaled, bound = [], 0.0
    for c in range(2):
        own = slice(first + c * part, first + (c + 1) * part)
        q = q_ref[here, own].reshape(rows, HDIM).astype(F32) * LOG2_SCALE
        high = q.astype(BF16)
        low = (q - high.astype(F32)).astype(BF16)
        scaled.append(jnp.concatenate([high, low], axis=1))
        bound = jnp.maximum(bound, jnp.max(jnp.sum(q * q, axis=1, keepdims=True)) * norm_sc[c])
    unshifted = bound <= SAFE_LOG2 * SAFE_LOG2

    def scores(c, j):
        return lax.dot_general(
            scaled[c], k_sc[c, pl.ds(j * block, block), :], CONTRACT_LAST, preferred_element_type=F32
        )

    def weigh(c, j, weights):
        return jnp.dot(weights.astype(BF16), v_sc[c, pl.ds(j * block, block), :], preferred_element_type=F32)

    def finish(sums):
        cond, uncond = (s[:, :HDIM] / s[:, HDIM:] for s in sums)
        o_ref[...] = (uncond + GUIDANCE * (cond - uncond)).astype(BF16).reshape(groups, part, HDIM)

    @pl.when(unshifted)
    def _():
        order = [(c, j) for c in range(2) for j in range(blocks)]
        sums = [None, None]
        ahead = scores(*order[0])
        for i, (c, j) in enumerate(order):
            now = ahead
            if i + 1 < len(order):
                ahead = scores(*order[i + 1])
            part_sum = weigh(c, j, jnp.exp2(now))
            sums[c] = part_sum if sums[c] is None else sums[c] + part_sum
        finish(sums)

    @pl.when(jnp.logical_not(unshifted))
    def _():
        sums = []
        for c in range(2):
            top = lax.fori_loop(
                0,
                blocks,
                lambda j, m: jnp.maximum(m, jnp.max(scores(c, j), axis=1, keepdims=True)),
                jnp.full((rows, 1), -jnp.inf, F32),
            )
            sums.append(
                lax.fori_loop(
                    0,
                    blocks,
                    lambda j, acc: acc + weigh(c, j, jnp.exp2(scores(c, j) - top)),
                    jnp.zeros((rows, 2 * HDIM), F32),
                )
            )
        finish(sums)


def attend(arrays, shard, part, first, groups, before=(), block=256):
    peers = arrays[0].shape[0]
    keys = peers * shard
    return pl.pallas_call(
        functools.partial(
            attend_kernel,
            arrays=len(arrays),
            shard=shard,
            part=part,
            first=first,
            groups=groups,
            block=block,
        ),
        grid=(peers // groups,),
        in_specs=[
            pl.BlockSpec(a.shape, lambda i: (0, 0, 0), pipeline_mode=pl.Buffered(1)) for a in arrays
        ]
        + [pl.BlockSpec(memory_space=pl.ANY) for _ in before],
        out_specs=pl.BlockSpec((groups, part, HDIM), lambda i: (i, len(before), 0)),
        out_shape=jax.ShapeDtypeStruct((peers, shard, HDIM), BF16),
        input_output_aliases={len(arrays): 0} if before else {},
        scratch_shapes=[
            pltpu.VMEM((2, keys, 2 * HDIM), BF16),
            pltpu.VMEM((2, keys, 2 * HDIM), BF16),
            pltpu.SMEM((2,), F32),
        ],
        compiler_params=pltpu.CompilerParams(vmem_limit_bytes=VMEM_LIMIT),
    )(*arrays, *before)


def step_kernel(steps, guided, latents, gain, *outs):
    denoised, moved = outs[-2:]
    heads = guided.shape[0]
    sigma_now = sigma_of(steps[0, 0])
    sigma_change = sigma_of(steps[0, 0] + 1) - sigma_now
    total = None
    for h in range(heads):
        g = guided[h].astype(F32)
        total = g * g if total is None else total + g * g
    mean = jnp.sum(total, axis=1, keepdims=True) / (heads * HDIM)
    scale = lax.rsqrt(mean + 1e-06)
    for h in range(heads):
        columns = slice(h * HDIM, (h + 1) * HDIM)
        velocity = guided[h].astype(F32) * scale * gain[:, columns].astype(F32)
        current = latents[0, 0, :, columns].astype(F32)
        denoised[0, 0, :, columns] = (current - sigma_now * velocity).astype(BF16)
        moved[:, columns] = (current + sigma_change * velocity).astype(BF16)


def token_rows(first, rows, width):
    return pl.BlockSpec((1, 1, rows, width), lambda i: (0, 0, first // rows, 0))


def sample_step(first, rows, steps_table, guided, latents, gain, before):
    heads = guided.shape[0]
    width = heads * HDIM
    return pl.pallas_call(
        step_kernel,
        grid=(1,),
        in_specs=[
            pl.BlockSpec(memory_space=pltpu.SMEM),
            pl.BlockSpec((heads, rows, HDIM), lambda i: (0, first // rows, 0)),
            token_rows(first, rows, width),
            pl.BlockSpec((1, width), lambda i: (0, 0)),
        ]
        + [pl.BlockSpec(memory_space=pl.ANY) for _ in before],
        out_specs=[token_rows(first, rows, width), pl.BlockSpec((rows, width), lambda i: (0, 0))],
        out_shape=[
            jax.ShapeDtypeStruct(latents.shape, BF16),
            jax.ShapeDtypeStruct((rows, width), BF16),
        ],
        input_output_aliases={4: 0} if before else {},
        compiler_params=pltpu.CompilerParams(vmem_limit_bytes=VMEM_LIMIT),
    )(steps_table, guided, latents, gain, *before)


def choose_kernel(flags, partner, moved, *outs):
    outs[-1][0, 0] = jnp.where(flags[0] == 1, partner[...], moved[...])


def choose(first, flags, partner, moved, shape, before):
    rows, width = moved.shape
    whole = pl.BlockSpec((rows, width), lambda i: (0, 0))
    return pl.pallas_call(
        choose_kernel,
        grid=(1,),
        in_specs=[pl.BlockSpec(memory_space=pltpu.SMEM), whole, whole]
        + [pl.BlockSpec(memory_space=pl.ANY) for _ in before],
        out_specs=token_rows(first, rows, width),
        out_shape=jax.ShapeDtypeStruct(shape, BF16),
        input_output_aliases={3: 0} if before else {},
        compiler_params=pltpu.CompilerParams(vmem_limit_bytes=VMEM_LIMIT),
    )(flags, partner, moved, *before)


def per_device(queries, keys, values, latents, gain, steps_table, flags):
    tokens = queries.shape[3]
    half = tokens // 2
    exchange = lambda a: lax.all_to_all(a, "seq", split_axis=0, concat_axis=0, tiled=True)
    after = lambda a, done: lax.optimization_barrier((a, done))[0]
    kvq = exchange(pack((keys, values, queries), ((0, tokens), (0, tokens), (0, half))))
    rest = exchange(after(pack((queries,), ((half, half),)), kvq))
    own = attend((kvq,), tokens, half, 4 * tokens, groups=16)
    own = attend((kvq, rest), tokens, half, 0, groups=16, before=(own,))
    guided = exchange(own)

    swap = lambda a: lax.ppermute(a, "expert", [(0, 1), (1, 0)])
    denoised, moved, partner, next_latents = (), [], [], ()
    for first in (0, half):
        denoised, part = sample_step(first, half, steps_table, guided, latents, gain, denoised)
        denoised = (denoised,)
        moved.append(part)
        partner.append(swap(part))
    for first, theirs, ours in zip((0, half), partner, moved):
        next_latents = (choose(first, flags, theirs, ours, latents.shape, next_latents),)
    return (*denoised, *next_latents)


def solution(mesh):
    placed = (
        P("expert", "batch", None, "seq", None),
        P("expert", "batch", None, "seq", None),
        P("expert", "batch", None, "seq", None),
        P("expert", "batch", "seq", None),
        P("expert", None),
        P("expert", "batch"),
        P("batch"),
    )
    return jax.shard_map(
        per_device,
        mesh=mesh,
        in_specs=placed,
        out_specs=(P("expert", "batch", "seq", None), P("expert", "batch", "seq", None)),
        check_vma=False,
    )
```

```python
import functools
import math

import jax
import jax.numpy as jnp
from jax import lax
from jax.experimental import pallas as pl
from jax.experimental.pallas import tpu as pltpu
from jax.sharding import PartitionSpec as P

HDIM = 128
STEPS = 40
GUIDANCE = 3.5
FLOW_SHIFT = 5.0
BF16 = jnp.bfloat16
F32 = jnp.float32

LOG2_SCALE = math.log2(math.e) / math.sqrt(HDIM)
SAFE_LOG2 = 100.0
CONTRACT_LAST = (((1,), (1,)), ((), ()))
VMEM_LIMIT = 32 << 20
ATTEND_VMEM = 52 << 20


def in_vmem(a):
    return pltpu.with_memory_space_constraint(a, pltpu.VMEM)


def sigma_of(step):
    level = 1.0 - step.astype(F32) / STEPS
    return FLOW_SHIFT * level / (1.0 + (FLOW_SHIFT - 1.0) * level)


def pack_kernel(*refs, spans):
    count = len(spans)
    sources, out, (ins, outs, in_sems, out_sems) = refs[:count], refs[count], refs[count + 1 :]
    heads = out.shape[0]
    pieces, at = [], 0
    for source, (first, rows) in zip(sources, spans):
        for branch in range(2):
            pieces.append((source.at[0, 0, branch, pl.ds(first, rows)], at, rows))
            at += rows
    reads = [
        pltpu.make_async_copy(source, ins.at[pl.ds(at, rows)], in_sems.at[n])
        for n, (source, at, rows) in enumerate(pieces)
    ]
    writes = [
        pltpu.make_async_copy(outs.at[:, pl.ds(at, rows)], out.at[:, pl.ds(at, rows)], out_sems.at[n])
        for n, (_, at, rows) in enumerate(pieces)
    ]
    for read in reads:
        read.start()
    for (_, at, rows), read, write in zip(pieces, reads, writes):
        read.wait()
        for h in range(heads):
            outs[h, at : at + rows] = ins[at : at + rows, h * HDIM : (h + 1) * HDIM]
        write.start()
    for write in writes:
        write.wait()


def pack(sources, spans):
    width = sources[0].shape[-1]
    heads = width // HDIM
    total = sum(2 * rows for _, rows in spans)
    count = 2 * len(spans)
    return pl.pallas_call(
        functools.partial(pack_kernel, spans=spans),
        in_specs=[pl.BlockSpec(memory_space=pltpu.HBM) for _ in sources],
        out_specs=pl.BlockSpec(memory_space=pltpu.HBM),
        out_shape=pltpu.HBM((heads, total, HDIM), BF16),
        scratch_shapes=[
            pltpu.VMEM((total, width), BF16),
            pltpu.VMEM((heads, total, HDIM), BF16),
            pltpu.SemaphoreType.DMA((count,)),
            pltpu.SemaphoreType.DMA((count,)),
        ],
        compiler_params=pltpu.CompilerParams(vmem_limit_bytes=VMEM_LIMIT),
    )(*(pltpu.with_memory_space_constraint(a, pltpu.HBM) for a in sources))


def attend_kernel(*refs, arrays, shard, part, first, groups):
    kv_ref, q_ref = refs[0], refs[arrays - 1]
    o_ref, norm_sc = refs[-2:]
    peers = kv_ref.shape[0]
    keys = peers * shard
    rows = groups * part

    def resident(n, at=slice(None)):
        return kv_ref[at, n * shard : (n + 1) * shard].reshape(-1, HDIM)

    def most(vectors):
        squares = jnp.dot(vectors * vectors, jnp.ones((HDIM, HDIM), BF16), preferred_element_type=F32)
        return jnp.max(squares) * 1.01

    @pl.when(pl.program_id(0) == 0)
    def _():
        for c in range(2):
            norm_sc[c] = most(resident(c))

    here = pl.ds(pl.program_id(0) * groups, groups)
    queries, bound = [], 0.0
    for c in range(2):
        q = q_ref[here, first + c * part : first + (c + 1) * part].reshape(rows, HDIM)
        queries.append(q)
        bound = jnp.maximum(bound, most(q) * norm_sc[c])
    unshifted = bound <= (SAFE_LOG2 / LOG2_SCALE) ** 2

    def scores(c, k):
        return lax.dot_general(queries[c], k, CONTRACT_LAST, preferred_element_type=F32) * LOG2_SCALE

    def lanes(weights):
        return sum(weights[:, at : at + HDIM] for at in range(0, weights.shape[1], HDIM))

    def weigh(weights, v):
        return jnp.dot(weights.astype(BF16), v, preferred_element_type=F32)

    def finish(sums, totals):
        cond, uncond = (s / jnp.sum(t, axis=1, keepdims=True) for s, t in zip(sums, totals))
        o_ref[...] = (uncond + GUIDANCE * (cond - uncond)).astype(BF16).reshape(groups, part, HDIM)

    @pl.when(unshifted)
    def _():
        ahead = [scores(c, resident(c)) for c in range(2)]
        weights = [jnp.exp2(a) for a in ahead]
        finish([weigh(w, resident(2 + c)) for c, w in enumerate(weights)], [lanes(w) for w in weights])

    @pl.when(jnp.logical_not(unshifted))
    def _():
        sums, totals = [], []
        per = 4
        for c in range(2):

            def highest(j, m):
                return jnp.maximum(m, jnp.max(scores(c, resident(c, pl.ds(j * per, per))), axis=1, keepdims=True))

            top = lax.fori_loop(0, peers // per, highest, jnp.full((rows, 1), -jnp.inf, F32))

            def add(j, carry):
                at = pl.ds(j * per, per)
                weights = jnp.exp2(scores(c, resident(c, at)) - top)
                return carry[0] + weigh(weights, resident(2 + c, at)), carry[1] + lanes(weights)

            zero = jnp.zeros((rows, HDIM), F32)
            total, count = lax.fori_loop(0, peers // per, add, (zero, zero))
            sums.append(total)
            totals.append(count)
        finish(sums, totals)


def attend(arrays, shard, span, first, groups, before=()):
    start, part = span
    peers = arrays[0].shape[0]
    return pl.pallas_call(
        functools.partial(
            attend_kernel,
            arrays=len(arrays),
            shard=shard,
            part=part,
            first=first,
            groups=groups,
        ),
        grid=(peers // groups,),
        in_specs=[pl.BlockSpec(memory_space=pltpu.VMEM) for _ in arrays]
        + [pl.BlockSpec(memory_space=pl.ANY) for _ in before],
        out_specs=pl.BlockSpec((groups, part, HDIM), lambda i: (i, start // part, 0)),
        out_shape=jax.ShapeDtypeStruct((peers, shard, HDIM), BF16),
        input_output_aliases={len(arrays): 0} if before else {},
        scratch_shapes=[pltpu.SMEM((2,), F32)],
        compiler_params=pltpu.CompilerParams(vmem_limit_bytes=ATTEND_VMEM),
    )(*(in_vmem(a) for a in arrays), *before)


def update_kernel(steps, guided, latents, gain, out, *, moves):
    heads = guided.shape[0]
    sigma_now = sigma_of(steps[0, 0])
    change = sigma_of(steps[0, 0] + 1) - sigma_now if moves else -sigma_now
    total = None
    for h in range(heads):
        g = guided[h].astype(F32)
        total = g * g if total is None else total + g * g
    mean = jnp.sum(total, axis=1, keepdims=True) / (heads * HDIM)
    scale = lax.rsqrt(mean + 1e-06)
    for h in range(heads):
        columns = slice(h * HDIM, (h + 1) * HDIM)
        velocity = guided[h].astype(F32) * scale * gain[:, columns].astype(F32)
        current = latents[0, 0, :, columns].astype(F32)
        out[0, 0, :, columns] = (current + change * velocity).astype(BF16)


def update(moves, steps_table, guided, latents, gain):
    whole = pl.BlockSpec(memory_space=pltpu.VMEM)
    return pl.pallas_call(
        functools.partial(update_kernel, moves=moves),
        in_specs=[pl.BlockSpec(memory_space=pltpu.SMEM), whole, whole, whole],
        out_specs=whole,
        out_shape=jax.ShapeDtypeStruct(latents.shape, BF16),
        compiler_params=pltpu.CompilerParams(vmem_limit_bytes=VMEM_LIMIT),
    )(steps_table, in_vmem(guided), in_vmem(latents), in_vmem(gain))


def choose_kernel(flags, partner, moved, out):
    out[...] = jnp.where(flags[0] == 1, partner[...], moved[...])


def choose(flags, partner, moved):
    whole = pl.BlockSpec(memory_space=pltpu.VMEM)
    return pl.pallas_call(
        choose_kernel,
        in_specs=[pl.BlockSpec(memory_space=pltpu.SMEM), whole, whole],
        out_specs=whole,
        out_shape=jax.ShapeDtypeStruct(moved.shape, BF16),
        compiler_params=pltpu.CompilerParams(vmem_limit_bytes=VMEM_LIMIT),
    )(flags, in_vmem(partner), in_vmem(moved))


def per_device(queries, keys, values, latents, gain, steps_table, flags):
    tokens = queries.shape[3]
    tail = tokens // 3
    head = tokens - tail
    exchange = lambda a: lax.all_to_all(a, "seq", split_axis=0, concat_axis=0, tiled=True)
    after = lambda a, done: lax.optimization_barrier((a, done))[0]
    kvq = exchange(pack((keys, values, queries), ((0, tokens), (0, tokens), (0, head))))
    rest = exchange(after(pack((queries,), ((head, tail),)), kvq))
    own = attend((kvq,), tokens, (0, head), 4 * tokens, groups=16)
    own = attend((kvq, rest), tokens, (head, tail), 0, groups=32, before=(own,))
    guided = exchange(own)

    moved = update(True, steps_table, guided, latents, gain)
    partner = lax.ppermute(moved, "expert", [(0, 1), (1, 0)])
    denoised = update(False, steps_table, guided, latents, gain)
    return (denoised, choose(flags, partner, moved))


def solution(mesh):
    placed = (
        P("expert", "batch", None, "seq", None),
        P("expert", "batch", None, "seq", None),
        P("expert", "batch", None, "seq", None),
        P("expert", "batch", "seq", None),
        P("expert", None),
        P("expert", "batch"),
        P("batch"),
    )
    return jax.shard_map(
        per_device,
        mesh=mesh,
        in_specs=placed,
        out_specs=(P("expert", "batch", "seq", None), P("expert", "batch", "seq", None)),
        check_vma=False,
    )
```

```python
import functools
import math

import jax
import jax.numpy as jnp
from jax import lax
from jax.experimental import pallas as pl
from jax.experimental.pallas import tpu as pltpu
from jax.sharding import Mesh
from jax.sharding import PartitionSpec as P

HDIM = 128
STEPS = 40
GUIDANCE = 3.5
FLOW_SHIFT = 5.0
BF16 = jnp.bfloat16
F32 = jnp.float32

Y, Z, CORE = SEQ = ("seq_y", "seq_z", "seq_core")
FAR = 4
NEAR = 8
LOG2_SCALE = math.log2(math.e) / math.sqrt(HDIM)
SAFE_LOG2 = 100.0
CONTRACT_LAST = (((1,), (1,)), ((), ()))
VMEM_LIMIT = 32 << 20
ATTEND_VMEM = 52 << 20


def in_vmem(a):
    return pltpu.with_memory_space_constraint(a, pltpu.VMEM)


def sigma_of(step):
    level = 1.0 - step.astype(F32) / STEPS
    return FLOW_SHIFT * level / (1.0 + (FLOW_SHIFT - 1.0) * level)


def pack_kernel(*refs, spans):
    count = len(spans)
    sources, out, (ins, outs, in_sems, out_sems) = refs[:count], refs[count], refs[count + 1 :]
    heads = out.shape[0]
    pieces, at = [], 0
    for source, (first, rows) in zip(sources, spans):
        for branch in range(2):
            pieces.append((source.at[0, 0, branch, pl.ds(first, rows)], at, rows))
            at += rows
    reads = [
        pltpu.make_async_copy(source, ins.at[pl.ds(at, rows)], in_sems.at[n])
        for n, (source, at, rows) in enumerate(pieces)
    ]
    writes = [
        pltpu.make_async_copy(outs.at[:, pl.ds(at, rows)], out.at[:, pl.ds(at, rows)], out_sems.at[n])
        for n, (_, at, rows) in enumerate(pieces)
    ]
    for read in reads:
        read.start()
    for (_, at, rows), read, write in zip(pieces, reads, writes):
        read.wait()
        for h in range(heads):
            outs[h, at : at + rows] = ins[at : at + rows, h * HDIM : (h + 1) * HDIM]
        write.start()
    for write in writes:
        write.wait()


def pack(sources, spans):
    width = sources[0].shape[-1]
    heads = width // HDIM
    total = sum(2 * rows for _, rows in spans)
    count = 2 * len(spans)
    return pl.pallas_call(
        functools.partial(pack_kernel, spans=spans),
        in_specs=[pl.BlockSpec(memory_space=pltpu.HBM) for _ in sources],
        out_specs=pl.BlockSpec(memory_space=pltpu.HBM),
        out_shape=pltpu.HBM((heads, total, HDIM), BF16),
        scratch_shapes=[
            pltpu.VMEM((total, width), BF16),
            pltpu.VMEM((heads, total, HDIM), BF16),
            pltpu.SemaphoreType.DMA((count,)),
            pltpu.SemaphoreType.DMA((count,)),
        ],
        compiler_params=pltpu.CompilerParams(vmem_limit_bytes=VMEM_LIMIT),
    )(*(pltpu.with_memory_space_constraint(a, pltpu.HBM) for a in sources))


def attend_kernel(place, *refs, arrays, shard, part, first, groups, normed):
    kv_ref, q_ref = refs[0], refs[arrays - 1]
    norms_in = refs[arrays] if normed else None
    *outs, norms = refs[-FAR - 1 :]
    peers = kv_ref.shape[0]
    rows = groups * NEAR * part

    def resident(n, at=slice(None)):
        return kv_ref[at, n * shard : (n + 1) * shard].reshape(-1, HDIM)

    def most(vectors):
        squares = jnp.dot(vectors * vectors, jnp.ones((HDIM, HDIM), BF16), preferred_element_type=F32)
        return jnp.max(squares) * 1.01

    @pl.when(pl.program_id(0) == 0)
    def _():
        for c in range(2):
            norms[c] = norms_in[c] if normed else most(resident(c))

    queries, bound = [], 0.0
    for c in range(2):
        own = slice(first + c * part, first + (c + 1) * part)
        pieces = []
        for g in range(groups):
            other = (pl.program_id(0) * groups + g) ^ place[0]
            for y in range(NEAR // 2):
                pieces.append(q_ref[pl.ds(y * 2 * FAR + other * 2, 2), own])
        q = jnp.concatenate(pieces, axis=0).reshape(rows, HDIM)
        queries.append(q)
        bound = jnp.maximum(bound, most(q) * norms[c])
    unshifted = bound <= (SAFE_LOG2 / LOG2_SCALE) ** 2

    def scores(c, k):
        return lax.dot_general(queries[c], k, CONTRACT_LAST, preferred_element_type=F32) * LOG2_SCALE

    def lanes(weights):
        return sum(weights[:, at : at + HDIM] for at in range(0, weights.shape[1], HDIM))

    def weigh(weights, v):
        return jnp.dot(weights.astype(BF16), v, preferred_element_type=F32)

    def finish(sums, totals):
        cond, uncond = (s / jnp.sum(t, axis=1, keepdims=True) for s, t in zip(sums, totals))
        guided = (uncond + GUIDANCE * (cond - uncond)).astype(BF16).reshape(groups, NEAR, part, HDIM)
        for step in range(FAR // groups):

            @pl.when(pl.program_id(0) == step)
            def _():
                for g in range(groups):
                    outs[step * groups + g][...] = guided[g]

    @pl.when(unshifted)
    def _():
        ahead = [scores(c, resident(c)) for c in range(2)]
        weights = [jnp.exp2(a) for a in ahead]
        finish([weigh(w, resident(2 + c)) for c, w in enumerate(weights)], [lanes(w) for w in weights])

    @pl.when(jnp.logical_not(unshifted))
    def _():
        sums, totals = [], []
        per = 4
        for c in range(2):

            def highest(j, m):
                return jnp.maximum(m, jnp.max(scores(c, resident(c, pl.ds(j * per, per))), axis=1, keepdims=True))

            top = lax.fori_loop(0, peers // per, highest, jnp.full((rows, 1), -jnp.inf, F32))

            def add(j, carry):
                at = pl.ds(j * per, per)
                weights = jnp.exp2(scores(c, resident(c, at)) - top)
                return carry[0] + weigh(weights, resident(2 + c, at)), carry[1] + lanes(weights)

            zero = jnp.zeros((rows, HDIM), F32)
            total, count = lax.fori_loop(0, peers // per, add, (zero, zero))
            sums.append(total)
            totals.append(count)
        finish(sums, totals)


def attend(place, arrays, shard, part, first, groups, norms=()):
    smem = pl.BlockSpec(memory_space=pltpu.SMEM)
    whole = pl.BlockSpec(memory_space=pltpu.VMEM)
    *outs, norms = pl.pallas_call(
        functools.partial(
            attend_kernel,
            arrays=len(arrays),
            shard=shard,
            part=part,
            first=first,
            groups=groups,
            normed=bool(norms),
        ),
        grid=(FAR // groups,),
        in_specs=[smem] + [whole for _ in arrays] + [smem for _ in norms],
        out_specs=[whole] * FAR + [smem],
        out_shape=[jax.ShapeDtypeStruct((NEAR, part, HDIM), BF16)] * FAR + [jax.ShapeDtypeStruct((2,), F32)],
        compiler_params=pltpu.CompilerParams(vmem_limit_bytes=ATTEND_VMEM),
    )(place, *(in_vmem(a) for a in arrays), *norms)
    return outs, norms


def regroup_kernel(*refs):
    *sources, out = refs
    for d, source in enumerate(sources):
        out[:, d] = source[...]


def regroup(pieces):
    near, part, _ = pieces[0].shape
    return pl.pallas_call(
        regroup_kernel,
        in_specs=[pl.BlockSpec(memory_space=pltpu.VMEM)] * len(pieces),
        out_specs=pl.BlockSpec(memory_space=pltpu.VMEM),
        out_shape=jax.ShapeDtypeStruct((near, len(pieces), part, HDIM), BF16),
        compiler_params=pltpu.CompilerParams(vmem_limit_bytes=VMEM_LIMIT),
    )(*(in_vmem(p) for p in pieces))


def changed_rows(place, guided, latents, gain, change, out, first):
    near, far, rows, _ = guided.shape
    heads = near * far

    def head(h):
        y, rest = divmod(h, 2 * far)
        z, core = divmod(rest, 2)
        return guided[2 * y + core, z ^ place[0]].astype(F32)

    total = None
    for h in range(heads):
        g = head(h)
        total = g * g if total is None else total + g * g
    mean = jnp.sum(total, axis=1, keepdims=True) / (heads * HDIM)
    scale = lax.rsqrt(mean + 1e-06)
    for h in range(heads):
        columns = slice(h * HDIM, (h + 1) * HDIM)
        velocity = head(h) * scale * gain[:, columns].astype(F32)
        current = latents[0, 0, first : first + rows, columns].astype(F32)
        out[:, columns] = (current + change * velocity).astype(BF16)


def move_kernel(place, steps, guided, latents, gain, out, *, first):
    change = sigma_of(steps[0, 0] + 1) - sigma_of(steps[0, 0])
    changed_rows(place, guided, latents, gain, change, out, first)


def denoise_kernel(place, steps, *refs):
    *parts, latents, gain, out = refs
    first = 0
    for guided in parts:
        rows = guided.shape[2]
        to = out.at[0, 0, pl.ds(first, rows)]
        changed_rows(place, guided, latents, gain, -sigma_of(steps[0, 0]), to, first)
        first += rows


def update(kernel, out_shape, place, steps_table, parts, latents, gain):
    smem = pl.BlockSpec(memory_space=pltpu.SMEM)
    whole = pl.BlockSpec(memory_space=pltpu.VMEM)
    return pl.pallas_call(
        kernel,
        in_specs=[smem, smem] + [whole] * (len(parts) + 2),
        out_specs=whole,
        out_shape=jax.ShapeDtypeStruct(out_shape, BF16),
        compiler_params=pltpu.CompilerParams(vmem_limit_bytes=VMEM_LIMIT),
    )(place, steps_table, *(in_vmem(a) for a in (*parts, latents, gain)))


def choose_kernel(flags, *refs):
    *pairs, out = refs
    count = len(pairs) // 2
    first = 0
    for partner, moved in zip(pairs[:count], pairs[count:]):
        rows = moved.shape[0]
        out[0, 0, first : first + rows] = jnp.where(flags[0] == 1, partner[...], moved[...])
        first += rows


def choose(flags, partner, moved, shape):
    whole = pl.BlockSpec(memory_space=pltpu.VMEM)
    operands = [*partner, *moved]
    return pl.pallas_call(
        choose_kernel,
        in_specs=[pl.BlockSpec(memory_space=pltpu.SMEM)] + [whole] * len(operands),
        out_specs=whole,
        out_shape=jax.ShapeDtypeStruct(shape, BF16),
        compiler_params=pltpu.CompilerParams(vmem_limit_bytes=VMEM_LIMIT),
    )(flags, *(in_vmem(a) for a in operands))


def per_device(queries, keys, values, latents, gain, steps_table, flags):
    tokens, width = queries.shape[3:]
    tail = tokens // 3
    head = tokens - tail
    place = lax.axis_index(Z).reshape(1).astype(jnp.int32)
    exchange = lambda a, axes: lax.all_to_all(a, axes, split_axis=0, concat_axis=0, tiled=True)
    together = lax.optimization_barrier

    def along_z(pieces):
        return [lax.ppermute(p, Z, [(i, i ^ d) for i in range(FAR)]) if d else p for d, p in enumerate(pieces)]

    kvq = exchange(pack((keys, values, queries), ((0, tokens), (0, tokens), (0, head))), SEQ)
    rest, _ = together((pack((queries,), ((head, tail),)), kvq))
    rest = exchange(rest, SEQ)
    own, norms = attend(place, (kvq,), tokens, head, 4 * tokens, groups=2)
    own, rest = together((own, rest))
    near = along_z(own)
    own, _ = attend(place, (kvq, rest), tokens, tail, 0, groups=4, norms=(norms,))
    near, own = together((near, own))
    far = along_z(own)
    guided_head = exchange(regroup(near), (Y, CORE))
    far, guided_head = together((far, guided_head))
    guided_tail = exchange(regroup(far), (Y, CORE))

    swap = lambda a: lax.ppermute(a, "expert", [(0, 1), (1, 0)])
    moved, partner = [], []
    for first, guided in ((0, guided_head), (head, guided_tail)):
        shape = (guided.shape[2], width)
        kernel = functools.partial(move_kernel, first=first)
        moved.append(update(kernel, shape, place, steps_table, (guided,), latents, gain))
        partner.append(swap(moved[-1]))
    parts = (guided_head, guided_tail)
    denoised = update(denoise_kernel, latents.shape, place, steps_table, parts, latents, gain)
    return (denoised, choose(flags, partner, moved, latents.shape))


def solution(mesh):
    sizes = (mesh.shape["expert"], mesh.shape["batch"], NEAR // 2, FAR, 2)
    torus = Mesh(mesh.devices.reshape(sizes), ("expert", "batch", *SEQ))
    placed = (
        P("expert", "batch", None, SEQ, None),
        P("expert", "batch", None, SEQ, None),
        P("expert", "batch", None, SEQ, None),
        P("expert", "batch", SEQ, None),
        P("expert", None),
        P("expert", "batch"),
        P("batch"),
    )
    return jax.shard_map(
        per_device,
        mesh=torus,
        in_specs=placed,
        out_specs=(P("expert", "batch", SEQ, None), P("expert", "batch", SEQ, None)),
        check_vma=False,
    )
```

```python
import functools
import math

import jax
import jax.numpy as jnp
from jax import lax
from jax.experimental import pallas as pl
from jax.experimental.pallas import tpu as pltpu
from jax.sharding import Mesh
from jax.sharding import PartitionSpec as P

HDIM = 128
STEPS = 40
GUIDANCE = 3.5
FLOW_SHIFT = 5.0
BF16 = jnp.bfloat16
F32 = jnp.float32

Y, Z, CORE = SEQ = ("seq_y", "seq_z", "seq_core")
FAR = 4
NEAR = 8
LOG2_SCALE = math.log2(math.e) / math.sqrt(HDIM)
SAFE_LOG2 = 100.0
CONTRACT_LAST = (((1,), (1,)), ((), ()))
VMEM_LIMIT = 32 << 20
ATTEND_VMEM = 40 << 20


def in_vmem(a):
    return pltpu.with_memory_space_constraint(a, pltpu.VMEM)


def in_hbm(a):
    return pltpu.with_memory_space_constraint(a, pltpu.HBM)


def sigma_of(step):
    level = 1.0 - step.astype(F32) / STEPS
    return FLOW_SHIFT * level / (1.0 + (FLOW_SHIFT - 1.0) * level)


def pack_kernel(*refs, branch):
    count = len(refs) - 5
    sources, out, (ins, outs, in_sems, out_sems) = refs[:count], refs[count], refs[count + 1 :]
    heads, total, _ = out.shape
    rows = total // count
    pieces = [(source.at[0, 0, branch], n * rows, rows) for n, source in enumerate(sources)]
    reads = [
        pltpu.make_async_copy(source, ins.at[pl.ds(at, rows)], in_sems.at[n])
        for n, (source, at, rows) in enumerate(pieces)
    ]
    writes = [
        pltpu.make_async_copy(outs.at[:, pl.ds(at, rows)], out.at[:, pl.ds(at, rows)], out_sems.at[n])
        for n, (_, at, rows) in enumerate(pieces)
    ]
    for read in reads:
        read.start()
    for (_, at, rows), read, write in zip(pieces, reads, writes):
        read.wait()
        for h in range(heads):
            outs[h, at : at + rows] = ins[at : at + rows, h * HDIM : (h + 1) * HDIM]
        write.start()
    for write in writes:
        write.wait()


def pack(branch, sources):
    tokens, width = sources[0].shape[3:]
    heads = width // HDIM
    count = len(sources)
    total = count * tokens
    return pl.pallas_call(
        functools.partial(pack_kernel, branch=branch),
        in_specs=[pl.BlockSpec(memory_space=pltpu.HBM) for _ in sources],
        out_specs=pl.BlockSpec(memory_space=pltpu.HBM),
        out_shape=pltpu.HBM((heads, total, HDIM), BF16),
        scratch_shapes=[
            pltpu.VMEM((total, width), BF16),
            pltpu.VMEM((heads, total, HDIM), BF16),
            pltpu.SemaphoreType.DMA((count,)),
            pltpu.SemaphoreType.DMA((count,)),
        ],
        compiler_params=pltpu.CompilerParams(vmem_limit_bytes=VMEM_LIMIT),
    )(*(in_hbm(a) for a in sources))


def attend_kernel(place, kvq_ref, *refs, shard, part, first, groups, normed, guide):
    refs = list(refs)
    norm_in = refs.pop(0) if normed else None
    cond_ref = refs.pop(0) if guide else None
    *outs, norm = refs
    peers = kvq_ref.shape[0]
    chunks = 2
    per_chunk = groups // chunks
    rows = per_chunk * NEAR * part
    step = pl.program_id(0)

    def resident(n, at=slice(None)):
        return kvq_ref[at, n * shard : (n + 1) * shard].reshape(-1, HDIM)

    def most(vectors):
        squares = jnp.dot(vectors * vectors, jnp.ones((HDIM, HDIM), BF16), preferred_element_type=F32)
        return jnp.max(squares) * 1.01

    @pl.when(step == 0)
    def _():
        norm[0] = norm_in[0] if normed else most(resident(0))

    queries, bound = [], 0.0
    for c in range(chunks):
        pieces = []
        for g in range(per_chunk):
            other = (step * groups + c * per_chunk + g) ^ place[0]
            for y in range(NEAR // 2):
                at = pl.ds(y * 2 * FAR + other * 2, 2)
                pieces.append(kvq_ref[at, 2 * shard + first : 2 * shard + first + part])
        q = jnp.concatenate(pieces, axis=0).reshape(rows, HDIM)
        queries.append(q)
        bound = jnp.maximum(bound, most(q) * norm[0])
    unshifted = bound <= (SAFE_LOG2 / LOG2_SCALE) ** 2

    def scores(q, k):
        return lax.dot_general(q, k, CONTRACT_LAST, preferred_element_type=F32) * LOG2_SCALE

    def lanes(weights):
        return sum(weights[:, at : at + HDIM] for at in range(0, weights.shape[1], HDIM))

    def weigh(weights, v):
        return jnp.dot(weights.astype(BF16), v, preferred_element_type=F32)

    def finish(c, total, count):
        attended = total / jnp.sum(count, axis=1, keepdims=True)
        shape = (per_chunk, NEAR, part, HDIM)
        if not guide:
            outs[0][c * per_chunk : (c + 1) * per_chunk] = attended.reshape(shape)
            return
        cond = cond_ref[c * per_chunk : (c + 1) * per_chunk].reshape(rows, HDIM)
        guided = (attended + GUIDANCE * (cond - attended)).astype(BF16).reshape(shape)
        for d in range(FAR):
            if d % groups // per_chunk == c:

                @pl.when(step == d // groups)
                def _():
                    outs[d][...] = guided[d % per_chunk]

    @pl.when(unshifted)
    def _():
        ahead = [scores(q, resident(0)) for q in queries]
        weights = [jnp.exp2(a) for a in ahead]
        sums = [weigh(w, resident(1)) for w in weights]
        for c in range(chunks):
            finish(c, sums[c], lanes(weights[c]))

    @pl.when(jnp.logical_not(unshifted))
    def _():
        per = 4
        for c, q in enumerate(queries):

            def highest(j, m):
                return jnp.maximum(m, jnp.max(scores(q, resident(0, pl.ds(j * per, per))), axis=1, keepdims=True))

            top = lax.fori_loop(0, peers // per, highest, jnp.full((rows, 1), -jnp.inf, F32))

            def add(j, carry):
                at = pl.ds(j * per, per)
                weights = jnp.exp2(scores(q, resident(0, at)) - top)
                return carry[0] + weigh(weights, resident(1, at)), carry[1] + lanes(weights)

            zero = jnp.zeros((rows, HDIM), F32)
            finish(c, *lax.fori_loop(0, peers // per, add, (zero, zero)))


def attend(place, kvq, part, first, groups, norm=(), cond=()):
    smem = pl.BlockSpec(memory_space=pltpu.SMEM)
    whole = pl.BlockSpec(memory_space=pltpu.VMEM)
    heads_spec = pl.BlockSpec(kvq.shape, lambda i: (0, 0, 0), pipeline_mode=pl.Buffered(1))
    if cond:
        heads_spec = whole
        out_specs = [whole] * FAR
        out_shape = [jax.ShapeDtypeStruct((NEAR, part, HDIM), BF16)] * FAR
    else:
        out_specs = [pl.BlockSpec((groups, NEAR, part, HDIM), lambda i: (i, 0, 0, 0))]
        out_shape = [pltpu.HBM((FAR, NEAR, part, HDIM), F32)]
    *outs, norm_out = pl.pallas_call(
        functools.partial(
            attend_kernel,
            shard=kvq.shape[1] // 3,
            part=part,
            first=first,
            groups=groups,
            normed=bool(norm),
            guide=bool(cond),
        ),
        grid=(FAR // groups,),
        in_specs=[smem, heads_spec]
        + [smem for _ in norm]
        + [pl.BlockSpec((groups, NEAR, part, HDIM), lambda i: (i, 0, first // part, 0)) for _ in cond],
        out_specs=out_specs + [smem],
        out_shape=out_shape + [jax.ShapeDtypeStruct((1,), F32)],
        compiler_params=pltpu.CompilerParams(vmem_limit_bytes=ATTEND_VMEM),
    )(place, in_vmem(kvq) if cond else in_hbm(kvq), *norm, *(in_hbm(a) for a in cond))
    return outs, norm_out


def regroup_kernel(*refs):
    *sources, out = refs
    for d, source in enumerate(sources):
        out[:, d] = source[...]


def regroup(pieces):
    near, part, _ = pieces[0].shape
    return pl.pallas_call(
        regroup_kernel,
        in_specs=[pl.BlockSpec(memory_space=pltpu.VMEM)] * len(pieces),
        out_specs=pl.BlockSpec(memory_space=pltpu.VMEM),
        out_shape=jax.ShapeDtypeStruct((near, len(pieces), part, HDIM), BF16),
        compiler_params=pltpu.CompilerParams(vmem_limit_bytes=VMEM_LIMIT),
    )(*(in_vmem(p) for p in pieces))


def changed_rows(place, guided, latents, gain, change, out, first):
    near, far, rows, _ = guided.shape
    heads = near * far

    def head(h):
        y, rest = divmod(h, 2 * far)
        z, core = divmod(rest, 2)
        return guided[2 * y + core, z ^ place[0]].astype(F32)

    total = None
    for h in range(heads):
        g = head(h)
        total = g * g if total is None else total + g * g
    mean = jnp.sum(total, axis=1, keepdims=True) / (heads * HDIM)
    scale = lax.rsqrt(mean + 1e-06)
    for h in range(heads):
        columns = slice(h * HDIM, (h + 1) * HDIM)
        velocity = head(h) * scale * gain[:, columns].astype(F32)
        current = latents[0, 0, first : first + rows, columns].astype(F32)
        out[:, columns] = (current + change * velocity).astype(BF16)


def move_kernel(place, steps, guided, latents, gain, out, *, first):
    change = sigma_of(steps[0, 0] + 1) - sigma_of(steps[0, 0])
    changed_rows(place, guided, latents, gain, change, out, first)


def denoise_kernel(place, steps, *refs):
    *parts, latents, gain, out = refs
    first = 0
    for guided in parts:
        rows = guided.shape[2]
        to = out.at[0, 0, pl.ds(first, rows)]
        changed_rows(place, guided, latents, gain, -sigma_of(steps[0, 0]), to, first)
        first += rows


def update(kernel, out_shape, place, steps_table, parts, latents, gain):
    smem = pl.BlockSpec(memory_space=pltpu.SMEM)
    whole = pl.BlockSpec(memory_space=pltpu.VMEM)
    return pl.pallas_call(
        kernel,
        in_specs=[smem, smem] + [whole] * (len(parts) + 2),
        out_specs=whole,
        out_shape=jax.ShapeDtypeStruct(out_shape, BF16),
        compiler_params=pltpu.CompilerParams(vmem_limit_bytes=VMEM_LIMIT),
    )(place, steps_table, *(in_vmem(a) for a in (*parts, latents, gain)))


def choose_kernel(flags, *refs):
    *pairs, out = refs
    count = len(pairs) // 2
    first = 0
    for partner, moved in zip(pairs[:count], pairs[count:]):
        rows = moved.shape[0]
        out[0, 0, first : first + rows] = jnp.where(flags[0] == 1, partner[...], moved[...])
        first += rows


def choose(flags, partner, moved, shape):
    whole = pl.BlockSpec(memory_space=pltpu.VMEM)
    operands = [*partner, *moved]
    return pl.pallas_call(
        choose_kernel,
        in_specs=[pl.BlockSpec(memory_space=pltpu.SMEM)] + [whole] * len(operands),
        out_specs=whole,
        out_shape=jax.ShapeDtypeStruct(shape, BF16),
        compiler_params=pltpu.CompilerParams(vmem_limit_bytes=VMEM_LIMIT),
    )(flags, *(in_vmem(a) for a in operands))


def per_device(queries, keys, values, latents, gain, steps_table, flags):
    tokens, width = queries.shape[3:]
    tail = tokens // 3
    head = tokens - tail
    place = lax.axis_index(Z).reshape(1).astype(jnp.int32)
    exchange = lambda a, axes: lax.all_to_all(a, axes, split_axis=0, concat_axis=0, tiled=True)
    together = lax.optimization_barrier

    def along_z(pieces):
        return [lax.ppermute(p, Z, [(i, i ^ d) for i in range(FAR)]) if d else p for d, p in enumerate(pieces)]

    sources = (keys, values, queries)
    cond_kvq = exchange(pack(0, sources), SEQ)
    packed, _ = together((pack(1, sources), cond_kvq))
    kvq = exchange(packed, SEQ)
    cond, _ = attend(place, cond_kvq, tokens, 0, groups=2)
    own, norm = attend(place, kvq, head, 0, groups=2, cond=cond)
    near = along_z(own)
    own, _ = attend(place, kvq, tail, head, groups=4, norm=(norm,), cond=cond)
    near, own = together((near, own))
    far = along_z(own)
    guided_head = exchange(regroup(near), (Y, CORE))
    far, guided_head = together((far, guided_head))
    guided_tail = exchange(regroup(far), (Y, CORE))

    swap = lambda a: lax.ppermute(a, "expert", [(0, 1), (1, 0)])
    moved, partner = [], []
    for first, guided in ((0, guided_head), (head, guided_tail)):
        shape = (guided.shape[2], width)
        kernel = functools.partial(move_kernel, first=first)
        moved.append(update(kernel, shape, place, steps_table, (guided,), latents, gain))
        partner.append(swap(moved[-1]))
    parts = (guided_head, guided_tail)
    denoised = update(denoise_kernel, latents.shape, place, steps_table, parts, latents, gain)
    return (denoised, choose(flags, partner, moved, latents.shape))


def solution(mesh):
    sizes = (mesh.shape["expert"], mesh.shape["batch"], NEAR // 2, FAR, 2)
    torus = Mesh(mesh.devices.reshape(sizes), ("expert", "batch", *SEQ))
    placed = (
        P("expert", "batch", None, SEQ, None),
        P("expert", "batch", None, SEQ, None),
        P("expert", "batch", None, SEQ, None),
        P("expert", "batch", SEQ, None),
        P("expert", None),
        P("expert", "batch"),
        P("batch"),
    )
    return jax.shard_map(
        per_device,
        mesh=torus,
        in_specs=placed,
        out_specs=(P("expert", "batch", SEQ, None), P("expert", "batch", SEQ, None)),
        check_vma=False,
    )
```

```python
import functools
import math

import jax
import jax.numpy as jnp
from jax import lax
from jax.experimental import pallas as pl
from jax.experimental.pallas import tpu as pltpu
from jax.sharding import Mesh
from jax.sharding import PartitionSpec as P

HDIM = 128
STEPS = 40
GUIDANCE = 3.5
FLOW_SHIFT = 5.0
BF16 = jnp.bfloat16
F32 = jnp.float32

Y, Z, CORE = SEQ = ("seq_y", "seq_z", "seq_core")
FAR = 4
NEAR = 8
LOG2_SCALE = math.log2(math.e) / math.sqrt(HDIM)
SAFE_LOG2 = 100.0
CONTRACT_LAST = (((1,), (1,)), ((), ()))
VMEM_LIMIT = 32 << 20
ATTEND_VMEM = 52 << 20


def in_vmem(a):
    return pltpu.with_memory_space_constraint(a, pltpu.VMEM)


def sigma_of(step):
    level = 1.0 - step.astype(F32) / STEPS
    return FLOW_SHIFT * level / (1.0 + (FLOW_SHIFT - 1.0) * level)


def pack_kernel(*refs, spans):
    count = len(spans)
    sources, out, (ins, outs, in_sems, out_sems) = refs[:count], refs[count], refs[count + 1 :]
    heads = out.shape[0]
    pieces, at = [], 0
    for source, (first, rows) in zip(sources, spans):
        for branch in range(2):
            pieces.append((source.at[0, 0, branch, pl.ds(first, rows)], at, rows))
            at += rows
    reads = [
        pltpu.make_async_copy(source, ins.at[pl.ds(at, rows)], in_sems.at[n])
        for n, (source, at, rows) in enumerate(pieces)
    ]
    writes = [
        pltpu.make_async_copy(outs.at[:, pl.ds(at, rows)], out.at[:, pl.ds(at, rows)], out_sems.at[n])
        for n, (_, at, rows) in enumerate(pieces)
    ]
    for read in reads:
        read.start()
    for (_, at, rows), read, write in zip(pieces, reads, writes):
        read.wait()
        for h in range(heads):
            outs[h, at : at + rows] = ins[at : at + rows, h * HDIM : (h + 1) * HDIM]
        write.start()
    for write in writes:
        write.wait()


def pack(sources, spans):
    width = sources[0].shape[-1]
    heads = width // HDIM
    total = sum(2 * rows for _, rows in spans)
    count = 2 * len(spans)
    return pl.pallas_call(
        functools.partial(pack_kernel, spans=spans),
        in_specs=[pl.BlockSpec(memory_space=pltpu.HBM) for _ in sources],
        out_specs=pl.BlockSpec(memory_space=pltpu.HBM),
        out_shape=pltpu.HBM((heads, total, HDIM), BF16),
        scratch_shapes=[
            pltpu.VMEM((total, width), BF16),
            pltpu.VMEM((heads, total, HDIM), BF16),
            pltpu.SemaphoreType.DMA((count,)),
            pltpu.SemaphoreType.DMA((count,)),
        ],
        compiler_params=pltpu.CompilerParams(vmem_limit_bytes=VMEM_LIMIT),
    )(*(pltpu.with_memory_space_constraint(a, pltpu.HBM) for a in sources))


def attend_kernel(place, *refs, arrays, shard, part, first, steps, groups, nearest, normed):
    kv_ref, q_ref = refs[0], refs[arrays - 1]
    norms_in = refs[arrays] if normed else None
    *outs, norms = refs[arrays + normed :]
    peers = kv_ref.shape[0]
    rows = groups * NEAR * part

    def resident(n, at=slice(None)):
        return kv_ref[at, n * shard : (n + 1) * shard].reshape(-1, HDIM)

    def most(vectors):
        squares = jnp.dot(vectors * vectors, jnp.ones((HDIM, HDIM), BF16), preferred_element_type=F32)
        return jnp.max(squares) * 1.01

    @pl.when(pl.program_id(0) == 0)
    def _():
        for c in range(2):
            norms[c] = norms_in[c] if normed else most(resident(c))

    queries, bound = [], 0.0
    for c in range(2):
        own = slice(first + c * part, first + (c + 1) * part)
        pieces = []
        for g in range(groups):
            other = (nearest + pl.program_id(0) * groups + g) ^ place[0]
            for y in range(NEAR // 2):
                pieces.append(q_ref[pl.ds(y * 2 * FAR + other * 2, 2), own])
        q = jnp.concatenate(pieces, axis=0).reshape(rows, HDIM)
        queries.append(q)
        bound = jnp.maximum(bound, most(q) * norms[c])
    unshifted = bound <= (SAFE_LOG2 / LOG2_SCALE) ** 2

    def scores(c, k):
        return lax.dot_general(queries[c], k, CONTRACT_LAST, preferred_element_type=F32) * LOG2_SCALE

    def lanes(weights):
        return sum(weights[:, at : at + HDIM] for at in range(0, weights.shape[1], HDIM))

    def weigh(weights, v):
        return jnp.dot(weights.astype(BF16), v, preferred_element_type=F32)

    def finish(sums, totals):
        cond, uncond = (s / jnp.sum(t, axis=1, keepdims=True) for s, t in zip(sums, totals))
        guided = (uncond + GUIDANCE * (cond - uncond)).astype(BF16).reshape(groups, NEAR, part, HDIM)
        for step in range(steps):

            @pl.when(pl.program_id(0) == step)
            def _():
                for g in range(groups):
                    outs[step * groups + g][...] = guided[g]

    @pl.when(unshifted)
    def _():
        ahead = [scores(c, resident(c)) for c in range(2)]
        weights = [jnp.exp2(a) for a in ahead]
        finish([weigh(w, resident(2 + c)) for c, w in enumerate(weights)], [lanes(w) for w in weights])

    @pl.when(jnp.logical_not(unshifted))
    def _():
        sums, totals = [], []
        per = 4
        for c in range(2):

            def highest(j, m):
                return jnp.maximum(m, jnp.max(scores(c, resident(c, pl.ds(j * per, per))), axis=1, keepdims=True))

            top = lax.fori_loop(0, peers // per, highest, jnp.full((rows, 1), -jnp.inf, F32))

            def add(j, carry):
                at = pl.ds(j * per, per)
                weights = jnp.exp2(scores(c, resident(c, at)) - top)
                return carry[0] + weigh(weights, resident(2 + c, at)), carry[1] + lanes(weights)

            zero = jnp.zeros((rows, HDIM), F32)
            total, count = lax.fori_loop(0, peers // per, add, (zero, zero))
            sums.append(total)
            totals.append(count)
        finish(sums, totals)


def attend(place, arrays, shard, part, first, span, groups, norms=()):
    smem = pl.BlockSpec(memory_space=pltpu.SMEM)
    whole = pl.BlockSpec(memory_space=pltpu.VMEM)
    nearest, count = span
    *outs, norms = pl.pallas_call(
        functools.partial(
            attend_kernel,
            arrays=len(arrays),
            shard=shard,
            part=part,
            first=first,
            steps=count // groups,
            groups=groups,
            nearest=nearest,
            normed=len(norms),
        ),
        grid=(count // groups,),
        in_specs=[smem] + [whole for _ in arrays] + [smem for _ in norms],
        out_specs=[whole] * count + [smem],
        out_shape=[jax.ShapeDtypeStruct((NEAR, part, HDIM), BF16)] * count + [jax.ShapeDtypeStruct((2,), F32)],
        compiler_params=pltpu.CompilerParams(vmem_limit_bytes=ATTEND_VMEM),
    )(place, *(in_vmem(a) for a in arrays), *norms)
    return outs, norms


def regroup_kernel(*refs):
    *sources, out = refs
    for d, source in enumerate(sources):
        out[:, d] = source[...]


def regroup(pieces):
    near, part, _ = pieces[0].shape
    return pl.pallas_call(
        regroup_kernel,
        in_specs=[pl.BlockSpec(memory_space=pltpu.VMEM)] * len(pieces),
        out_specs=pl.BlockSpec(memory_space=pltpu.VMEM),
        out_shape=jax.ShapeDtypeStruct((near, len(pieces), part, HDIM), BF16),
        compiler_params=pltpu.CompilerParams(vmem_limit_bytes=VMEM_LIMIT),
    )(*(in_vmem(p) for p in pieces))


def changed_rows(place, guided, latents, gain, change, out, first):
    near, far, rows, _ = guided.shape
    heads = near * far

    def head(h):
        y, rest = divmod(h, 2 * far)
        z, core = divmod(rest, 2)
        return guided[2 * y + core, z ^ place[0]].astype(F32)

    total = None
    for h in range(heads):
        g = head(h)
        total = g * g if total is None else total + g * g
    mean = jnp.sum(total, axis=1, keepdims=True) / (heads * HDIM)
    scale = lax.rsqrt(mean + 1e-06)
    for h in range(heads):
        columns = slice(h * HDIM, (h + 1) * HDIM)
        velocity = head(h) * scale * gain[:, columns].astype(F32)
        current = latents[0, 0, first : first + rows, columns].astype(F32)
        out[:, columns] = (current + change * velocity).astype(BF16)


def move_kernel(place, steps, guided, latents, gain, out, *, first):
    change = sigma_of(steps[0, 0] + 1) - sigma_of(steps[0, 0])
    changed_rows(place, guided, latents, gain, change, out, first)


def denoise_kernel(place, steps, *refs):
    *parts, latents, gain, out = refs
    first = 0
    for guided in parts:
        rows = guided.shape[2]
        to = out.at[0, 0, pl.ds(first, rows)]
        changed_rows(place, guided, latents, gain, -sigma_of(steps[0, 0]), to, first)
        first += rows


def update(kernel, out_shape, place, steps_table, parts, latents, gain):
    smem = pl.BlockSpec(memory_space=pltpu.SMEM)
    whole = pl.BlockSpec(memory_space=pltpu.VMEM)
    return pl.pallas_call(
        kernel,
        in_specs=[smem, smem] + [whole] * (len(parts) + 2),
        out_specs=whole,
        out_shape=jax.ShapeDtypeStruct(out_shape, BF16),
        compiler_params=pltpu.CompilerParams(vmem_limit_bytes=VMEM_LIMIT),
    )(place, steps_table, *(in_vmem(a) for a in (*parts, latents, gain)))


def choose_kernel(flags, *refs):
    *pairs, out = refs
    count = len(pairs) // 2
    first = 0
    for partner, moved in zip(pairs[:count], pairs[count:]):
        rows = moved.shape[0]
        out[0, 0, first : first + rows] = jnp.where(flags[0] == 1, partner[...], moved[...])
        first += rows


def choose(flags, partner, moved, shape):
    whole = pl.BlockSpec(memory_space=pltpu.VMEM)
    operands = [*partner, *moved]
    return pl.pallas_call(
        choose_kernel,
        in_specs=[pl.BlockSpec(memory_space=pltpu.SMEM)] + [whole] * len(operands),
        out_specs=whole,
        out_shape=jax.ShapeDtypeStruct(shape, BF16),
        compiler_params=pltpu.CompilerParams(vmem_limit_bytes=VMEM_LIMIT),
    )(flags, *(in_vmem(a) for a in operands))


def per_device(queries, keys, values, latents, gain, steps_table, flags):
    tokens, width = queries.shape[3:]
    half = tokens // 2
    place = lax.axis_index(Z).reshape(1).astype(jnp.int32)
    exchange = lambda a, axes: lax.all_to_all(a, axes, split_axis=0, concat_axis=0, tiled=True)
    together = lax.optimization_barrier

    def along_z(pieces, nearest=0):
        routes = [[(i, i ^ d) for i in range(FAR)] for d in range(nearest, nearest + len(pieces))]
        return [p if r[0] == (0, 0) else lax.ppermute(p, Z, r) for p, r in zip(pieces, routes)]

    kvq = exchange(pack((keys, values, queries), ((0, tokens), (0, tokens), (0, half))), SEQ)
    rest, _ = together((pack((queries,), ((half, half),)), kvq))
    rest = exchange(rest, SEQ)
    own, norms = attend(place, (kvq,), tokens, half, 4 * tokens, (0, FAR), groups=2)
    near = along_z(own)
    other = lambda nearest: attend(
        place, (kvq, rest), tokens, half, 0, (nearest, FAR // 2), groups=2, norms=(norms,)
    )[0]
    far_low = other(0)
    near, far_low = together((near, far_low))
    guided_head = exchange(regroup(near), (Y, CORE))
    far = along_z(far_low) + along_z(other(FAR // 2), FAR // 2)
    far, guided_head = together((far, guided_head))
    guided_tail = exchange(regroup(far), (Y, CORE))

    swap = lambda a: lax.ppermute(a, "expert", [(0, 1), (1, 0)])
    moved, partner = [], []
    for first, guided in ((0, guided_head), (half, guided_tail)):
        shape = (guided.shape[2], width)
        kernel = functools.partial(move_kernel, first=first)
        moved.append(update(kernel, shape, place, steps_table, (guided,), latents, gain))
        partner.append(swap(moved[-1]))
    parts = (guided_head, guided_tail)
    denoised = update(denoise_kernel, latents.shape, place, steps_table, parts, latents, gain)
    return (denoised, choose(flags, partner, moved, latents.shape))


def solution(mesh):
    sizes = (mesh.shape["expert"], mesh.shape["batch"], NEAR // 2, FAR, 2)
    torus = Mesh(mesh.devices.reshape(sizes), ("expert", "batch", *SEQ))
    placed = (
        P("expert", "batch", None, SEQ, None),
        P("expert", "batch", None, SEQ, None),
        P("expert", "batch", None, SEQ, None),
        P("expert", "batch", SEQ, None),
        P("expert", None),
        P("expert", "batch"),
        P("batch"),
    )
    return jax.shard_map(
        per_device,
        mesh=torus,
        in_specs=placed,
        out_specs=(P("expert", "batch", SEQ, None), P("expert", "batch", SEQ, None)),
        check_vma=False,
    )
```

```python
import functools
import math

import jax
import jax.numpy as jnp
from jax import lax
from jax.experimental import pallas as pl
from jax.experimental.pallas import tpu as pltpu
from jax.sharding import Mesh
from jax.sharding import PartitionSpec as P

HDIM = 128
STEPS = 40
GUIDANCE = 3.5
FLOW_SHIFT = 5.0
BF16 = jnp.bfloat16
F32 = jnp.float32

Y, Z, CORE = SEQ = ("seq_y", "seq_z", "seq_core")
FAR = 4
NEAR = 8
LOG2_SCALE = math.log2(math.e) / math.sqrt(HDIM)
SAFE_LOG2 = 100.0
CONTRACT_LAST = (((1,), (1,)), ((), ()))
VMEM_LIMIT = 32 << 20
ATTEND_VMEM = 52 << 20


def in_vmem(a):
    return pltpu.with_memory_space_constraint(a, pltpu.VMEM)


def sigma_of(step):
    level = 1.0 - step.astype(F32) / STEPS
    return FLOW_SHIFT * level / (1.0 + (FLOW_SHIFT - 1.0) * level)


def pack_kernel(*refs, spans):
    count = len(spans)
    sources, out, (ins, outs, in_sems, out_sems) = refs[:count], refs[count], refs[count + 1 :]
    heads = out.shape[0]
    pieces, at = [], 0
    for source, (first, rows) in zip(sources, spans):
        for branch in range(2):
            pieces.append((source.at[0, 0, branch, pl.ds(first, rows)], at, rows))
            at += rows
    reads = [
        pltpu.make_async_copy(source, ins.at[pl.ds(at, rows)], in_sems.at[n])
        for n, (source, at, rows) in enumerate(pieces)
    ]
    writes = [
        pltpu.make_async_copy(outs.at[:, pl.ds(at, rows)], out.at[:, pl.ds(at, rows)], out_sems.at[n])
        for n, (_, at, rows) in enumerate(pieces)
    ]
    for read in reads:
        read.start()
    for (_, at, rows), read, write in zip(pieces, reads, writes):
        read.wait()
        for h in range(heads):
            outs[h, at : at + rows] = ins[at : at + rows, h * HDIM : (h + 1) * HDIM]
        write.start()
    for write in writes:
        write.wait()


def pack(sources, spans):
    width = sources[0].shape[-1]
    heads = width // HDIM
    total = sum(2 * rows for _, rows in spans)
    count = 2 * len(spans)
    return pl.pallas_call(
        functools.partial(pack_kernel, spans=spans),
        in_specs=[pl.BlockSpec(memory_space=pltpu.HBM) for _ in sources],
        out_specs=pl.BlockSpec(memory_space=pltpu.HBM),
        out_shape=pltpu.HBM((heads, total, HDIM), BF16),
        scratch_shapes=[
            pltpu.VMEM((total, width), BF16),
            pltpu.VMEM((heads, total, HDIM), BF16),
            pltpu.SemaphoreType.DMA((count,)),
            pltpu.SemaphoreType.DMA((count,)),
        ],
        compiler_params=pltpu.CompilerParams(vmem_limit_bytes=VMEM_LIMIT),
    )(*(pltpu.with_memory_space_constraint(a, pltpu.HBM) for a in sources))


def attend_kernel(place, *refs, arrays, shard, part, first, groups, normed, joined):
    kv_ref, q_ref = refs[0], refs[arrays - 1]
    norms_in = refs[arrays] if normed else None
    *outs, norms = refs[arrays + normed :]
    peers = kv_ref.shape[0]
    rows = groups * NEAR * part

    def resident(n, at=slice(None)):
        return kv_ref[at, n * shard : (n + 1) * shard].reshape(-1, HDIM)

    def most(vectors):
        squares = jnp.dot(vectors * vectors, jnp.ones((HDIM, HDIM), BF16), preferred_element_type=F32)
        return jnp.max(squares) * 1.01

    @pl.when(pl.program_id(0) == 0)
    def _():
        for c in range(2):
            norms[c] = norms_in[c] if normed else most(resident(c))

    queries, bound = [], 0.0
    for c in range(2):
        own = slice(first + c * part, first + (c + 1) * part)
        pieces = []
        for g in range(groups):
            other = pl.program_id(0) * groups + g
            if not joined:
                other = other ^ place[0]
            for y in range(NEAR // 2):
                pieces.append(q_ref[pl.ds(y * 2 * FAR + other * 2, 2), own])
        q = jnp.concatenate(pieces, axis=0).reshape(rows, HDIM)
        queries.append(q)
        bound = jnp.maximum(bound, most(q) * norms[c])
    unshifted = bound <= (SAFE_LOG2 / LOG2_SCALE) ** 2

    def scores(c, k):
        return lax.dot_general(queries[c], k, CONTRACT_LAST, preferred_element_type=F32) * LOG2_SCALE

    def lanes(weights):
        return sum(weights[:, at : at + HDIM] for at in range(0, weights.shape[1], HDIM))

    def weigh(weights, v):
        return jnp.dot(weights.astype(BF16), v, preferred_element_type=F32)

    def finish(sums, totals):
        cond, uncond = (s / jnp.sum(t, axis=1, keepdims=True) for s, t in zip(sums, totals))
        guided = (uncond + GUIDANCE * (cond - uncond)).astype(BF16).reshape(groups, NEAR, part, HDIM)
        if joined:
            outs[0][pl.ds(pl.program_id(0) * groups, groups)] = guided
            return
        for step in range(FAR // groups):

            @pl.when(pl.program_id(0) == step)
            def _():
                for g in range(groups):
                    outs[step * groups + g][...] = guided[g]

    @pl.when(unshifted)
    def _():
        ahead = [scores(c, resident(c)) for c in range(2)]
        weights = [jnp.exp2(a) for a in ahead]
        finish([weigh(w, resident(2 + c)) for c, w in enumerate(weights)], [lanes(w) for w in weights])

    @pl.when(jnp.logical_not(unshifted))
    def _():
        sums, totals = [], []
        per = 4
        for c in range(2):

            def highest(j, m):
                return jnp.maximum(m, jnp.max(scores(c, resident(c, pl.ds(j * per, per))), axis=1, keepdims=True))

            top = lax.fori_loop(0, peers // per, highest, jnp.full((rows, 1), -jnp.inf, F32))

            def add(j, carry):
                at = pl.ds(j * per, per)
                weights = jnp.exp2(scores(c, resident(c, at)) - top)
                return carry[0] + weigh(weights, resident(2 + c, at)), carry[1] + lanes(weights)

            zero = jnp.zeros((rows, HDIM), F32)
            total, count = lax.fori_loop(0, peers // per, add, (zero, zero))
            sums.append(total)
            totals.append(count)
        finish(sums, totals)


def attend(place, arrays, shard, part, first, groups, joined, norms=()):
    smem = pl.BlockSpec(memory_space=pltpu.SMEM)
    whole = pl.BlockSpec(memory_space=pltpu.VMEM)
    shapes = [(FAR, NEAR, part, HDIM)] if joined else [(NEAR, part, HDIM)] * FAR
    *outs, norms = pl.pallas_call(
        functools.partial(
            attend_kernel,
            arrays=len(arrays),
            shard=shard,
            part=part,
            first=first,
            groups=groups,
            normed=len(norms),
            joined=joined,
        ),
        grid=(FAR // groups,),
        in_specs=[smem] + [whole for _ in arrays] + [smem for _ in norms],
        out_specs=[whole] * len(shapes) + [smem],
        out_shape=[jax.ShapeDtypeStruct(a, BF16) for a in shapes] + [jax.ShapeDtypeStruct((2,), F32)],
        compiler_params=pltpu.CompilerParams(vmem_limit_bytes=ATTEND_VMEM),
    )(place, *(in_vmem(a) for a in arrays), *norms)
    return outs, norms


def regroup_kernel(place, *refs):
    *sources, out = refs
    if len(sources) == 1:
        for z in range(FAR):
            out[:, z] = sources[0][z]
        return
    for d, source in enumerate(sources):
        out[:, pl.ds(d ^ place[0], 1)] = source[...][:, None]


def regroup(place, pieces):
    part = pieces[0].shape[-2]
    return pl.pallas_call(
        regroup_kernel,
        in_specs=[pl.BlockSpec(memory_space=pltpu.SMEM)] + [pl.BlockSpec(memory_space=pltpu.VMEM)] * len(pieces),
        out_specs=pl.BlockSpec(memory_space=pltpu.VMEM),
        out_shape=jax.ShapeDtypeStruct((NEAR, FAR, part, HDIM), BF16),
        compiler_params=pltpu.CompilerParams(vmem_limit_bytes=VMEM_LIMIT),
    )(place, *(in_vmem(p) for p in pieces))


def changed_rows(guided, latents, gain, change, out, first):
    near, far, rows, _ = guided.shape
    heads = near * far

    def head(h):
        y, rest = divmod(h, 2 * far)
        z, core = divmod(rest, 2)
        return guided[2 * y + core, z].astype(F32)

    total = None
    for h in range(heads):
        g = head(h)
        total = g * g if total is None else total + g * g
    mean = jnp.sum(total, axis=1, keepdims=True) / (heads * HDIM)
    scale = lax.rsqrt(mean + 1e-06)
    for h in range(heads):
        columns = slice(h * HDIM, (h + 1) * HDIM)
        velocity = head(h) * scale * gain[:, columns].astype(F32)
        current = latents[0, 0, first : first + rows, columns].astype(F32)
        out[:, columns] = (current + change * velocity).astype(BF16)


def move_kernel(steps, guided, latents, gain, out, *, first):
    change = sigma_of(steps[0, 0] + 1) - sigma_of(steps[0, 0])
    changed_rows(guided, latents, gain, change, out, first)


def denoise_kernel(steps, *refs):
    *parts, latents, gain, out = refs
    first = 0
    for guided in parts:
        rows = guided.shape[2]
        to = out.at[0, 0, pl.ds(first, rows)]
        changed_rows(guided, latents, gain, -sigma_of(steps[0, 0]), to, first)
        first += rows


def update(kernel, out_shape, steps_table, parts, latents, gain):
    smem = pl.BlockSpec(memory_space=pltpu.SMEM)
    whole = pl.BlockSpec(memory_space=pltpu.VMEM)
    return pl.pallas_call(
        kernel,
        in_specs=[smem] + [whole] * (len(parts) + 2),
        out_specs=whole,
        out_shape=jax.ShapeDtypeStruct(out_shape, BF16),
        compiler_params=pltpu.CompilerParams(vmem_limit_bytes=VMEM_LIMIT),
    )(steps_table, *(in_vmem(a) for a in (*parts, latents, gain)))


def choose_kernel(flags, *refs):
    *pairs, out = refs
    count = len(pairs) // 2
    first = 0
    for partner, moved in zip(pairs[:count], pairs[count:]):
        rows = moved.shape[0]
        out[0, 0, first : first + rows] = jnp.where(flags[0] == 1, partner[...], moved[...])
        first += rows


def choose(flags, partner, moved, shape):
    whole = pl.BlockSpec(memory_space=pltpu.VMEM)
    operands = [*partner, *moved]
    return pl.pallas_call(
        choose_kernel,
        in_specs=[pl.BlockSpec(memory_space=pltpu.SMEM)] + [whole] * len(operands),
        out_specs=whole,
        out_shape=jax.ShapeDtypeStruct(shape, BF16),
        compiler_params=pltpu.CompilerParams(vmem_limit_bytes=VMEM_LIMIT),
    )(flags, *(in_vmem(a) for a in operands))


def per_device(queries, keys, values, latents, gain, steps_table, flags):
    tokens, width = queries.shape[3:]
    tail = tokens // 3
    head = tokens - tail
    place = lax.axis_index(Z).reshape(1).astype(jnp.int32)
    exchange = lambda a, axes: lax.all_to_all(a, axes, split_axis=0, concat_axis=0, tiled=True)
    together = lax.optimization_barrier

    def along_z(pieces):
        out = list(pieces)
        for d in (2, 1, 3):
            out[d] = lax.ppermute(pieces[d], Z, [(i, i ^ d) for i in range(FAR)])
        return out

    kvq = exchange(pack((keys, values, queries), ((0, tokens), (0, tokens), (0, head))), SEQ)
    rest, _ = together((pack((queries,), ((head, tail),)), kvq))
    rest = exchange(rest, SEQ)
    own, norms = attend(place, (kvq,), tokens, head, 4 * tokens, groups=2, joined=True)
    own, rest = together((own[0], rest))
    near = exchange(own, Z)
    own, _ = attend(place, (kvq, rest), tokens, tail, 0, groups=4, joined=False, norms=(norms,))
    near, own = together((near, own))
    far = along_z(own)
    guided_head = exchange(regroup(place, (near,)), (Y, CORE))
    far, guided_head = together((far, guided_head))
    guided_tail = exchange(regroup(place, far), (Y, CORE))

    swap = lambda a: lax.ppermute(a, "expert", [(0, 1), (1, 0)])
    moved, partner = [], []
    for first, guided in ((0, guided_head), (head, guided_tail)):
        shape = (guided.shape[2], width)
        kernel = functools.partial(move_kernel, first=first)
        moved.append(update(kernel, shape, steps_table, (guided,), latents, gain))
        partner.append(swap(moved[-1]))
    parts = (guided_head, guided_tail)
    denoised = update(denoise_kernel, latents.shape, steps_table, parts, latents, gain)
    return (denoised, choose(flags, partner, moved, latents.shape))


def solution(mesh):
    sizes = (mesh.shape["expert"], mesh.shape["batch"], NEAR // 2, FAR, 2)
    torus = Mesh(mesh.devices.reshape(sizes), ("expert", "batch", *SEQ))
    placed = (
        P("expert", "batch", None, SEQ, None),
        P("expert", "batch", None, SEQ, None),
        P("expert", "batch", None, SEQ, None),
        P("expert", "batch", SEQ, None),
        P("expert", None),
        P("expert", "batch"),
        P("batch"),
    )
    return jax.shard_map(
        per_device,
        mesh=torus,
        in_specs=placed,
        out_specs=(P("expert", "batch", SEQ, None), P("expert", "batch", SEQ, None)),
        check_vma=False,
    )
```

```python
import functools
import math

import jax
import jax.numpy as jnp
from jax import lax
from jax.experimental import pallas as pl
from jax.experimental.pallas import tpu as pltpu
from jax.sharding import Mesh
from jax.sharding import PartitionSpec as P

HDIM = 128
STEPS = 40
GUIDANCE = 3.5
FLOW_SHIFT = 5.0
BF16 = jnp.bfloat16
F32 = jnp.float32

Y, Z, CORE = SEQ = ("seq_y", "seq_z", "seq_core")
FAR = 4
NEAR = 8
LOG2_SCALE = math.log2(math.e) / math.sqrt(HDIM)
SAFE_LOG2 = 100.0
CONTRACT_LAST = (((1,), (1,)), ((), ()))
VMEM_LIMIT = 32 << 20
ATTEND_VMEM = 52 << 20


def in_vmem(a):
    return pltpu.with_memory_space_constraint(a, pltpu.VMEM)


def sigma_of(step):
    level = 1.0 - step.astype(F32) / STEPS
    return FLOW_SHIFT * level / (1.0 + (FLOW_SHIFT - 1.0) * level)


def pack_kernel(*refs, spans):
    count = len(spans)
    sources, out, (ins, outs, in_sems, out_sems) = refs[:count], refs[count], refs[count + 1 :]
    heads = out.shape[0]
    pieces, at = [], 0
    for source, (first, rows) in zip(sources, spans):
        for branch in range(2):
            pieces.append((source.at[0, 0, branch, pl.ds(first, rows)], at, rows))
            at += rows
    reads = [
        pltpu.make_async_copy(source, ins.at[pl.ds(at, rows)], in_sems.at[n])
        for n, (source, at, rows) in enumerate(pieces)
    ]
    writes = [
        pltpu.make_async_copy(outs.at[:, pl.ds(at, rows)], out.at[:, pl.ds(at, rows)], out_sems.at[n])
        for n, (_, at, rows) in enumerate(pieces)
    ]
    for read in reads:
        read.start()
    for (_, at, rows), read, write in zip(pieces, reads, writes):
        read.wait()
        for h in range(heads):
            outs[h, at : at + rows] = ins[at : at + rows, h * HDIM : (h + 1) * HDIM]
        write.start()
    for write in writes:
        write.wait()


def pack(sources, spans):
    width = sources[0].shape[-1]
    heads = width // HDIM
    total = sum(2 * rows for _, rows in spans)
    count = 2 * len(spans)
    return pl.pallas_call(
        functools.partial(pack_kernel, spans=spans),
        in_specs=[pl.BlockSpec(memory_space=pltpu.HBM) for _ in sources],
        out_specs=pl.BlockSpec(memory_space=pltpu.HBM),
        out_shape=pltpu.HBM((heads, total, HDIM), BF16),
        scratch_shapes=[
            pltpu.VMEM((total, width), BF16),
            pltpu.VMEM((heads, total, HDIM), BF16),
            pltpu.SemaphoreType.DMA((count,)),
            pltpu.SemaphoreType.DMA((count,)),
        ],
        compiler_params=pltpu.CompilerParams(vmem_limit_bytes=VMEM_LIMIT),
    )(*(pltpu.with_memory_space_constraint(a, pltpu.HBM) for a in sources))


def attend_kernel(place, *refs, arrays, shard, part, first, groups, normed):
    kv_ref, q_ref = refs[0], refs[arrays - 1]
    norms_in = refs[arrays] if normed else None
    *outs, norms = refs[-FAR - 1 :]
    peers = kv_ref.shape[0]
    rows = groups * NEAR * part

    def resident(n, at=slice(None)):
        return kv_ref[at, n * shard : (n + 1) * shard].reshape(-1, HDIM)

    def most(vectors):
        squares = jnp.dot(vectors * vectors, jnp.ones((HDIM, HDIM), BF16), preferred_element_type=F32)
        return jnp.max(squares) * 1.01

    @pl.when(pl.program_id(0) == 0)
    def _():
        for c in range(2):
            norms[c] = norms_in[c] if normed else most(resident(c))

    queries, bound = [], 0.0
    for c in range(2):
        own = slice(first + c * part, first + (c + 1) * part)
        pieces = []
        for g in range(groups):
            other = (pl.program_id(0) * groups + g) ^ place[0]
            for y in range(NEAR // 2):
                pieces.append(q_ref[pl.ds(y * 2 * FAR + other * 2, 2), own])
        q = jnp.concatenate(pieces, axis=0).reshape(rows, HDIM)
        queries.append(q)
        bound = jnp.maximum(bound, most(q) * norms[c])
    unshifted = bound <= (SAFE_LOG2 / LOG2_SCALE) ** 2

    def scores(c, k):
        return lax.dot_general(queries[c], k, CONTRACT_LAST, preferred_element_type=F32) * LOG2_SCALE

    def lanes(weights):
        return sum(weights[:, at : at + HDIM] for at in range(0, weights.shape[1], HDIM))

    def weigh(weights, v):
        return jnp.dot(weights.astype(BF16), v, preferred_element_type=F32)

    def finish(sums, totals):
        cond, uncond = (s / jnp.sum(t, axis=1, keepdims=True) for s, t in zip(sums, totals))
        guided = (uncond + GUIDANCE * (cond - uncond)).astype(BF16).reshape(groups, NEAR, part, HDIM)
        for step in range(FAR // groups):

            @pl.when(pl.program_id(0) == step)
            def _():
                for g in range(groups):
                    outs[step * groups + g][...] = guided[g]

    @pl.when(unshifted)
    def _():
        ahead = [scores(c, resident(c)) for c in range(2)]
        weights = [jnp.exp2(a) for a in ahead]
        finish([weigh(w, resident(2 + c)) for c, w in enumerate(weights)], [lanes(w) for w in weights])

    @pl.when(jnp.logical_not(unshifted))
    def _():
        sums, totals = [], []
        per = 4
        for c in range(2):

            def highest(j, m):
                return jnp.maximum(m, jnp.max(scores(c, resident(c, pl.ds(j * per, per))), axis=1, keepdims=True))

            top = lax.fori_loop(0, peers // per, highest, jnp.full((rows, 1), -jnp.inf, F32))

            def add(j, carry):
                at = pl.ds(j * per, per)
                weights = jnp.exp2(scores(c, resident(c, at)) - top)
                return carry[0] + weigh(weights, resident(2 + c, at)), carry[1] + lanes(weights)

            zero = jnp.zeros((rows, HDIM), F32)
            total, count = lax.fori_loop(0, peers // per, add, (zero, zero))
            sums.append(total)
            totals.append(count)
        finish(sums, totals)


def attend(place, arrays, shard, part, first, groups, norms=()):
    smem = pl.BlockSpec(memory_space=pltpu.SMEM)
    whole = pl.BlockSpec(memory_space=pltpu.VMEM)
    *outs, norms = pl.pallas_call(
        functools.partial(
            attend_kernel,
            arrays=len(arrays),
            shard=shard,
            part=part,
            first=first,
            groups=groups,
            normed=bool(norms),
        ),
        grid=(FAR // groups,),
        in_specs=[smem] + [whole for _ in arrays] + [smem for _ in norms],
        out_specs=[whole] * FAR + [smem],
        out_shape=[jax.ShapeDtypeStruct((NEAR, part, HDIM), BF16)] * FAR + [jax.ShapeDtypeStruct((2,), F32)],
        compiler_params=pltpu.CompilerParams(vmem_limit_bytes=ATTEND_VMEM),
    )(place, *(in_vmem(a) for a in arrays), *norms)
    return outs, norms


def regroup_kernel(*refs):
    *sources, out = refs
    for d, source in enumerate(sources):
        out[:, d] = source[...]


def regroup(pieces):
    near, part, _ = pieces[0].shape
    return pl.pallas_call(
        regroup_kernel,
        in_specs=[pl.BlockSpec(memory_space=pltpu.VMEM)] * len(pieces),
        out_specs=pl.BlockSpec(memory_space=pltpu.VMEM),
        out_shape=jax.ShapeDtypeStruct((near, len(pieces), part, HDIM), BF16),
        compiler_params=pltpu.CompilerParams(vmem_limit_bytes=VMEM_LIMIT),
    )(*(in_vmem(p) for p in pieces))


def changed_rows(place, guided, latents, gain, change, out, first):
    near, far, rows, _ = guided.shape
    heads = near * far

    def head(h):
        y, rest = divmod(h, 2 * far)
        z, core = divmod(rest, 2)
        return guided[2 * y + core, z ^ place[0]].astype(F32)

    total = None
    for h in range(heads):
        g = head(h)
        total = g * g if total is None else total + g * g
    mean = jnp.sum(total, axis=1, keepdims=True) / (heads * HDIM)
    scale = lax.rsqrt(mean + 1e-06)
    for h in range(heads):
        columns = slice(h * HDIM, (h + 1) * HDIM)
        velocity = head(h) * scale * gain[:, columns].astype(F32)
        current = latents[0, 0, first : first + rows, columns].astype(F32)
        out[:, columns] = (current + change * velocity).astype(BF16)


def move_kernel(place, steps, guided, latents, gain, out, *, first):
    change = sigma_of(steps[0, 0] + 1) - sigma_of(steps[0, 0])
    changed_rows(place, guided, latents, gain, change, out, first)


def denoise_kernel(place, steps, *refs):
    *parts, latents, gain, out = refs
    first = 0
    for guided in parts:
        rows = guided.shape[2]
        to = out.at[0, 0, pl.ds(first, rows)]
        changed_rows(place, guided, latents, gain, -sigma_of(steps[0, 0]), to, first)
        first += rows


def update(kernel, out_shape, place, steps_table, parts, latents, gain):
    smem = pl.BlockSpec(memory_space=pltpu.SMEM)
    whole = pl.BlockSpec(memory_space=pltpu.VMEM)
    return pl.pallas_call(
        kernel,
        in_specs=[smem, smem] + [whole] * (len(parts) + 2),
        out_specs=whole,
        out_shape=jax.ShapeDtypeStruct(out_shape, BF16),
        compiler_params=pltpu.CompilerParams(vmem_limit_bytes=VMEM_LIMIT),
    )(place, steps_table, *(in_vmem(a) for a in (*parts, latents, gain)))


def choose_kernel(flags, *refs):
    *pairs, out = refs
    count = len(pairs) // 2
    first = 0
    for partner, moved in zip(pairs[:count], pairs[count:]):
        rows = moved.shape[0]
        out[0, 0, first : first + rows] = jnp.where(flags[0] == 1, partner[...], moved[...])
        first += rows


def choose(flags, partner, moved, shape):
    whole = pl.BlockSpec(memory_space=pltpu.VMEM)
    operands = [*partner, *moved]
    return pl.pallas_call(
        choose_kernel,
        in_specs=[pl.BlockSpec(memory_space=pltpu.SMEM)] + [whole] * len(operands),
        out_specs=whole,
        out_shape=jax.ShapeDtypeStruct(shape, BF16),
        compiler_params=pltpu.CompilerParams(vmem_limit_bytes=VMEM_LIMIT),
    )(flags, *(in_vmem(a) for a in operands))


def per_device(queries, keys, values, latents, gain, steps_table, flags):
    tokens, width = queries.shape[3:]
    tail = tokens // 2
    head = tokens - tail
    place = lax.axis_index(Z).reshape(1).astype(jnp.int32)
    exchange = lambda a, axes: lax.all_to_all(a, axes, split_axis=0, concat_axis=0, tiled=True)
    together = lax.optimization_barrier

    def along_z(pieces):
        return [lax.ppermute(p, Z, [(i, i ^ d) for i in range(FAR)]) if d else p for d, p in enumerate(pieces)]

    kvq = exchange(pack((keys, values, queries), ((0, tokens), (0, tokens), (0, head))), SEQ)
    rest, _ = together((pack((queries,), ((head, tail),)), kvq))
    rest = exchange(rest, SEQ)
    own, norms = attend(place, (kvq,), tokens, head, 4 * tokens, groups=2)
    own, rest = together((own, rest))
    near = along_z(own)
    own, _ = attend(place, (kvq, rest), tokens, tail, 0, groups=2, norms=(norms,))
    near, own = together((near, own))
    far = along_z(own)
    guided_head = exchange(regroup(near), (Y, CORE))
    far, guided_head = together((far, guided_head))
    guided_tail = exchange(regroup(far), (Y, CORE))

    swap = lambda a: lax.ppermute(a, "expert", [(0, 1), (1, 0)])
    moved, partner = [], []
    for first, guided in ((0, guided_head), (head, guided_tail)):
        shape = (guided.shape[2], width)
        kernel = functools.partial(move_kernel, first=first)
        moved.append(update(kernel, shape, place, steps_table, (guided,), latents, gain))
        partner.append(swap(moved[-1]))
    parts = (guided_head, guided_tail)
    denoised = update(denoise_kernel, latents.shape, place, steps_table, parts, latents, gain)
    return (denoised, choose(flags, partner, moved, latents.shape))


def solution(mesh):
    sizes = (mesh.shape["expert"], mesh.shape["batch"], NEAR // 2, FAR, 2)
    torus = Mesh(mesh.devices.reshape(sizes), ("expert", "batch", *SEQ))
    placed = (
        P("expert", "batch", None, SEQ, None),
        P("expert", "batch", None, SEQ, None),
        P("expert", "batch", None, SEQ, None),
        P("expert", "batch", SEQ, None),
        P("expert", None),
        P("expert", "batch"),
        P("batch"),
    )
    return jax.shard_map(
        per_device,
        mesh=torus,
        in_specs=placed,
        out_specs=(P("expert", "batch", SEQ, None), P("expert", "batch", SEQ, None)),
        check_vma=False,
    )
```

```python
import functools
import math

import jax
import jax.numpy as jnp
from jax import lax
from jax.experimental import pallas as pl
from jax.experimental.pallas import tpu as pltpu
from jax.sharding import Mesh
from jax.sharding import PartitionSpec as P

HDIM = 128
STEPS = 40
GUIDANCE = 3.5
FLOW_SHIFT = 5.0
BF16 = jnp.bfloat16
F32 = jnp.float32

Y, Z, CORE = SEQ = ("seq_y", "seq_z", "seq_core")
FAR = 4
NEAR = 8
LOG2_SCALE = math.log2(math.e) / math.sqrt(HDIM)
SAFE_LOG2 = 100.0
CONTRACT_LAST = (((1,), (1,)), ((), ()))
VMEM_LIMIT = 32 << 20
ATTEND_VMEM = 52 << 20


def in_vmem(a):
    return pltpu.with_memory_space_constraint(a, pltpu.VMEM)


def sigma_of(step):
    level = 1.0 - step.astype(F32) / STEPS
    return FLOW_SHIFT * level / (1.0 + (FLOW_SHIFT - 1.0) * level)


def pack_kernel(*refs, spans):
    count = len(spans)
    sources, out, (ins, outs, in_sems, out_sems) = refs[:count], refs[count], refs[count + 1 :]
    heads = out.shape[0]
    pieces, at = [], 0
    for source, (first, rows) in zip(sources, spans):
        for branch in range(2):
            for start in (first, first + rows // 2):
                pieces.append((source.at[0, 0, branch, pl.ds(start, rows // 2)], at, rows // 2))
                at += rows // 2
    reads = [
        pltpu.make_async_copy(source, ins.at[pl.ds(at, rows)], in_sems.at[n])
        for n, (source, at, rows) in enumerate(pieces)
    ]
    writes = [
        pltpu.make_async_copy(outs.at[:, pl.ds(at, rows)], out.at[:, pl.ds(at, rows)], out_sems.at[n])
        for n, (_, at, rows) in enumerate(pieces)
    ]
    for read in reads:
        read.start()
    for (_, at, rows), read, write in zip(pieces, reads, writes):
        read.wait()
        for h in range(heads):
            outs[h, at : at + rows] = ins[at : at + rows, h * HDIM : (h + 1) * HDIM]
        write.start()
    for write in writes:
        write.wait()


def pack(sources, spans):
    width = sources[0].shape[-1]
    heads = width // HDIM
    total = sum(2 * rows for _, rows in spans)
    count = 4 * len(spans)
    return pl.pallas_call(
        functools.partial(pack_kernel, spans=spans),
        in_specs=[pl.BlockSpec(memory_space=pltpu.HBM) for _ in sources],
        out_specs=pl.BlockSpec(memory_space=pltpu.HBM),
        out_shape=pltpu.HBM((heads, total, HDIM), BF16),
        scratch_shapes=[
            pltpu.VMEM((total, width), BF16),
            pltpu.VMEM((heads, total, HDIM), BF16),
            pltpu.SemaphoreType.DMA((count,)),
            pltpu.SemaphoreType.DMA((count,)),
        ],
        compiler_params=pltpu.CompilerParams(vmem_limit_bytes=VMEM_LIMIT),
    )(*(pltpu.with_memory_space_constraint(a, pltpu.HBM) for a in sources))


def attend_kernel(place, *refs, arrays, shard, part, first, groups, normed):
    kv_ref, q_ref = refs[0], refs[arrays - 1]
    norms_in = refs[arrays] if normed else None
    *outs, norms = refs[-FAR - 1 :]
    peers = kv_ref.shape[0]
    rows = groups * NEAR * part

    def resident(n, at=slice(None)):
        return kv_ref[at, n * shard : (n + 1) * shard].reshape(-1, HDIM)

    def most(vectors):
        squares = jnp.dot(vectors * vectors, jnp.ones((HDIM, HDIM), BF16), preferred_element_type=F32)
        return jnp.max(squares) * 1.01

    @pl.when(pl.program_id(0) == 0)
    def _():
        for c in range(2):
            norms[c] = norms_in[c] if normed else most(resident(c))

    queries, bound = [], 0.0
    for c in range(2):
        own = slice(first + c * part, first + (c + 1) * part)
        pieces = []
        for g in range(groups):
            other = (pl.program_id(0) * groups + g) ^ place[0]
            for y in range(NEAR // 2):
                pieces.append(q_ref[pl.ds(y * 2 * FAR + other * 2, 2), own])
        q = jnp.concatenate(pieces, axis=0).reshape(rows, HDIM)
        queries.append(q)
        bound = jnp.maximum(bound, most(q) * norms[c])
    unshifted = bound <= (SAFE_LOG2 / LOG2_SCALE) ** 2

    def scores(c, k):
        return lax.dot_general(queries[c], k, CONTRACT_LAST, preferred_element_type=F32) * LOG2_SCALE

    def lanes(weights):
        return sum(weights[:, at : at + HDIM] for at in range(0, weights.shape[1], HDIM))

    def weigh(weights, v):
        return jnp.dot(weights.astype(BF16), v, preferred_element_type=F32)

    def finish(sums, totals):
        cond, uncond = (s / jnp.sum(t, axis=1, keepdims=True) for s, t in zip(sums, totals))
        guided = (uncond + GUIDANCE * (cond - uncond)).astype(BF16).reshape(groups, NEAR, part, HDIM)
        for step in range(FAR // groups):

            @pl.when(pl.program_id(0) == step)
            def _():
                for g in range(groups):
                    outs[step * groups + g][...] = guided[g]

    @pl.when(unshifted)
    def _():
        ahead = [scores(c, resident(c)) for c in range(2)]
        weights = [jnp.exp2(a) for a in ahead]
        finish([weigh(w, resident(2 + c)) for c, w in enumerate(weights)], [lanes(w) for w in weights])

    @pl.when(jnp.logical_not(unshifted))
    def _():
        sums, totals = [], []
        per = 4
        for c in range(2):

            def highest(j, m):
                return jnp.maximum(m, jnp.max(scores(c, resident(c, pl.ds(j * per, per))), axis=1, keepdims=True))

            top = lax.fori_loop(0, peers // per, highest, jnp.full((rows, 1), -jnp.inf, F32))

            def add(j, carry):
                at = pl.ds(j * per, per)
                weights = jnp.exp2(scores(c, resident(c, at)) - top)
                return carry[0] + weigh(weights, resident(2 + c, at)), carry[1] + lanes(weights)

            zero = jnp.zeros((rows, HDIM), F32)
            total, count = lax.fori_loop(0, peers // per, add, (zero, zero))
            sums.append(total)
            totals.append(count)
        finish(sums, totals)


def attend(place, arrays, shard, part, first, groups, norms=()):
    smem = pl.BlockSpec(memory_space=pltpu.SMEM)
    whole = pl.BlockSpec(memory_space=pltpu.VMEM)
    *outs, norms = pl.pallas_call(
        functools.partial(
            attend_kernel,
            arrays=len(arrays),
            shard=shard,
            part=part,
            first=first,
            groups=groups,
            normed=bool(norms),
        ),
        grid=(FAR // groups,),
        in_specs=[smem] + [whole for _ in arrays] + [smem for _ in norms],
        out_specs=[whole] * FAR + [smem],
        out_shape=[jax.ShapeDtypeStruct((NEAR, part, HDIM), BF16)] * FAR + [jax.ShapeDtypeStruct((2,), F32)],
        compiler_params=pltpu.CompilerParams(vmem_limit_bytes=ATTEND_VMEM),
    )(place, *(in_vmem(a) for a in arrays), *norms)
    return outs, norms


def regroup_kernel(*refs):
    *sources, out = refs
    for d, source in enumerate(sources):
        out[:, d] = source[...]


def regroup(pieces):
    near, part, _ = pieces[0].shape
    return pl.pallas_call(
        regroup_kernel,
        in_specs=[pl.BlockSpec(memory_space=pltpu.VMEM)] * len(pieces),
        out_specs=pl.BlockSpec(memory_space=pltpu.VMEM),
        out_shape=jax.ShapeDtypeStruct((near, len(pieces), part, HDIM), BF16),
        compiler_params=pltpu.CompilerParams(vmem_limit_bytes=VMEM_LIMIT),
    )(*(in_vmem(p) for p in pieces))


def changed_rows(place, guided, latents, gain, change, out, first):
    near, far, rows, _ = guided.shape
    heads = near * far

    def head(h):
        y, rest = divmod(h, 2 * far)
        z, core = divmod(rest, 2)
        return guided[2 * y + core, z ^ place[0]].astype(F32)

    total = None
    for h in range(heads):
        g = head(h)
        total = g * g if total is None else total + g * g
    mean = jnp.sum(total, axis=1, keepdims=True) / (heads * HDIM)
    scale = lax.rsqrt(mean + 1e-06)
    for h in range(heads):
        columns = slice(h * HDIM, (h + 1) * HDIM)
        velocity = head(h) * scale * gain[:, columns].astype(F32)
        current = latents[0, 0, first : first + rows, columns].astype(F32)
        out[:, columns] = (current + change * velocity).astype(BF16)


def move_kernel(place, steps, guided, latents, gain, out, *, first):
    change = sigma_of(steps[0, 0] + 1) - sigma_of(steps[0, 0])
    changed_rows(place, guided, latents, gain, change, out, first)


def denoise_kernel(place, steps, *refs):
    *parts, latents, gain, out = refs
    first = 0
    for guided in parts:
        rows = guided.shape[2]
        to = out.at[0, 0, pl.ds(first, rows)]
        changed_rows(place, guided, latents, gain, -sigma_of(steps[0, 0]), to, first)
        first += rows


def update(kernel, out_shape, place, steps_table, parts, latents, gain):
    smem = pl.BlockSpec(memory_space=pltpu.SMEM)
    whole = pl.BlockSpec(memory_space=pltpu.VMEM)
    return pl.pallas_call(
        kernel,
        in_specs=[smem, smem] + [whole] * (len(parts) + 2),
        out_specs=whole,
        out_shape=jax.ShapeDtypeStruct(out_shape, BF16),
        compiler_params=pltpu.CompilerParams(vmem_limit_bytes=VMEM_LIMIT),
    )(place, steps_table, *(in_vmem(a) for a in (*parts, latents, gain)))


def choose_kernel(flags, *refs):
    *pairs, out = refs
    count = len(pairs) // 2
    first = 0
    for partner, moved in zip(pairs[:count], pairs[count:]):
        rows = moved.shape[0]
        out[0, 0, first : first + rows] = jnp.where(flags[0] == 1, partner[...], moved[...])
        first += rows


def choose(flags, partner, moved, shape):
    whole = pl.BlockSpec(memory_space=pltpu.VMEM)
    operands = [*partner, *moved]
    return pl.pallas_call(
        choose_kernel,
        in_specs=[pl.BlockSpec(memory_space=pltpu.SMEM)] + [whole] * len(operands),
        out_specs=whole,
        out_shape=jax.ShapeDtypeStruct(shape, BF16),
        compiler_params=pltpu.CompilerParams(vmem_limit_bytes=VMEM_LIMIT),
    )(flags, *(in_vmem(a) for a in operands))


def per_device(queries, keys, values, latents, gain, steps_table, flags):
    tokens, width = queries.shape[3:]
    tail = tokens // 3
    head = tokens - tail
    place = lax.axis_index(Z).reshape(1).astype(jnp.int32)
    exchange = lambda a, axes: lax.all_to_all(a, axes, split_axis=0, concat_axis=0, tiled=True)
    together = lax.optimization_barrier

    def along_z(pieces):
        return [lax.ppermute(p, Z, [(i, i ^ d) for i in range(FAR)]) if d else p for d, p in enumerate(pieces)]

    kvq = exchange(pack((keys, values, queries), ((0, tokens), (0, tokens), (0, head))), SEQ)
    rest, _ = together((pack((queries,), ((head, tail),)), kvq))
    rest = exchange(rest, SEQ)
    own, norms = attend(place, (kvq,), tokens, head, 4 * tokens, groups=2)
    own, rest = together((own, rest))
    near = along_z(own)
    own, _ = attend(place, (kvq, rest), tokens, tail, 0, groups=4, norms=(norms,))
    near, own = together((near, own))
    far = along_z(own)
    guided_head = exchange(regroup(near), (Y, CORE))
    far, guided_head = together((far, guided_head))
    guided_tail = exchange(regroup(far), (Y, CORE))

    swap = lambda a: lax.ppermute(a, "expert", [(0, 1), (1, 0)])
    moved, partner = [], []
    for first, guided in ((0, guided_head), (head, guided_tail)):
        shape = (guided.shape[2], width)
        kernel = functools.partial(move_kernel, first=first)
        moved.append(update(kernel, shape, place, steps_table, (guided,), latents, gain))
        partner.append(swap(moved[-1]))
    parts = (guided_head, guided_tail)
    denoised = update(denoise_kernel, latents.shape, place, steps_table, parts, latents, gain)
    return (denoised, choose(flags, partner, moved, latents.shape))


def solution(mesh):
    sizes = (mesh.shape["expert"], mesh.shape["batch"], NEAR // 2, FAR, 2)
    torus = Mesh(mesh.devices.reshape(sizes), ("expert", "batch", *SEQ))
    placed = (
        P("expert", "batch", None, SEQ, None),
        P("expert", "batch", None, SEQ, None),
        P("expert", "batch", None, SEQ, None),
        P("expert", "batch", SEQ, None),
        P("expert", None),
        P("expert", "batch"),
        P("batch"),
    )
    return jax.shard_map(
        per_device,
        mesh=torus,
        in_specs=placed,
        out_specs=(P("expert", "batch", SEQ, None), P("expert", "batch", SEQ, None)),
        check_vma=False,
    )
```
